256 devices in a mesh: ev: 4 (over y), slab: 64 (over x, z, core).
Axes of the slice: x: 4, y: 4, z: 8, core: 2. Of those that a mesh axis runs over, the one named last changes fastest.
Arguments:
- kernels: float32 [8192, 32, 128], P(('ev', 'slab')), may hold values from -1 to 1
- block_ids: int32 [8192, 32], P(('ev', 'slab')), may hold values from 0 to 65535, as said below
- delays: float32 [8192], P(('ev', 'slab')), may hold values from -240 to 240
Outputs:
- solution: float32 [512, 128, 128], P('slab')
The draws below stay inside these ranges and needn't reach their ends.
Inputs may be any that keep to these rules, and one draw needn't show every extreme that they name: `block_ids`: block b is column (b // 128, b % 128) and lies in slab b // 1024. Of the 1024 ids of one device's rays, exactly 16 lie in each slab; ids may repeat.
All inputs are finite; a program needn't handle non-finite values.
Results may differ from the reference program's by a relative error of at most 0.0001.
Values sent between devices are 32-bit elements; how exact they have to be, the bound alone decides.
No kernel may reach another device: no remote copies, remote signals or barrier semaphores. Data moves between devices by JAX's collectives and lax.ppermute only.
A program may use at most 64 MiB of HBM per device.

```python
import jax
import jax.numpy as jnp
from jax import lax

BLOCK = 128
K = 32
RAYS_DEV = 32
CX = 8
NY = 128
ITERS = 2
RAYS = 8192
NX = 512


def draw_block_ids(key, part):
    slab_count = NX // CX
    per_device = RAYS_DEV * K
    per_slab = per_device // slab_count
    device_count = RAYS // RAYS_DEV
    cells_slab = CX * NY
    owners_base = jnp.repeat(jnp.arange(slab_count, dtype=jnp.int32), per_slab)
    key_list = jax.random.split(jax.random.fold_in(key, 11), device_count)

    def shuffle(one_key):
        return jax.random.permutation(one_key, owners_base)
    owners = jax.vmap(shuffle)(key_list)
    inside = jax.random.randint(jax.random.fold_in(key, 12), (device_count, per_device), 0, cells_slab, dtype=jnp.int32)
    first_low = jnp.argmax(owners == 0, axis=1)
    first_high = jnp.argmax(owners == slab_count - 1, axis=1)
    rows_index = jnp.arange(device_count)
    inside = inside.at[rows_index, first_high].set(cells_slab - 1)
    inside = inside.at[rows_index, first_low].set(0)
    block_list = owners * cells_slab + inside
    return block_list.reshape(RAYS, K).astype(jnp.int32)


def draw_kernels(key, part):
    slab_count = NX // CX
    cells_slab = CX * NY
    ids = draw_block_ids(key, part)
    owner = (ids // cells_slab).astype(jnp.float32)
    ramp = 1.0 + 2.0 * owner / max(slab_count - 1, 1)
    base_key = jax.random.fold_in(key, 31)
    scale = (K * BLOCK) ** (-0.5)
    values = jnp.clip(jax.random.normal(base_key, (RAYS, K, BLOCK), jnp.float32), -6.0, 6.0)
    factor = ramp
    return jnp.clip(values * factor[:, :, None] * scale, -1.0, 1.0).astype(jnp.float32)


def draw_delays(key, part):
    ramp = 1.0 + 2.0 * jnp.arange(RAYS, dtype=jnp.float32) / (RAYS - 1)
    noise = jnp.clip(jax.random.normal(key, (RAYS,), jnp.float32), -4.5, 4.5)
    return 16.0 * ramp * noise


def setup_inputs(seed: int = 0) -> dict:
    streams_of = jax.random.split(jax.random.key(seed), 4)
    return {
        "kernels": draw_kernels(jax.random.fold_in(streams_of[3], 71), 0),
        "block_ids": draw_block_ids(jax.random.fold_in(streams_of[3], 71), 0),
        "delays": draw_delays(jax.random.fold_in(streams_of[3], 71), 0),
    }


damping = 0.3
norm_epsilon = 1e-06

def laplace_grid(field_in):
    rolled = jnp.roll(field_in, 1, 0) + jnp.roll(field_in, -1, 0)
    beside_all = jnp.pad(field_in, ((0, 0), (1, 1), (1, 1)))
    beside = rolled + beside_all[:, 2:, 1:-1] + beside_all[:, :-2, 1:-1] + beside_all[:, 1:-1, 2:] + beside_all[:, 1:-1, :-2]
    return 6.0 * field_in - beside

def ray_apply(model_in, block_ids, kernels):
    groups = RAYS // RAYS_DEV
    table = model_in.reshape(NX * NY, BLOCK)

    def per_group(pair):
        group_ids, group_kernels = pair
        return lax.optimization_barrier(jnp.sum(table[group_ids] * group_kernels, axis=(1, 2)))
    result = lax.map(per_group, (block_ids.reshape(groups, RAYS_DEV, K), kernels.reshape(groups, RAYS_DEV, K, BLOCK)))
    return result.reshape(RAYS)

def ray_transpose(ray_weights, block_ids, kernels):
    groups = RAYS // RAYS_DEV

    def add_group(summed, triple):
        group_ids, group_kernels, group_weights = triple
        terms = group_kernels * group_weights[:, None, None]
        return (summed.at[group_ids.reshape(-1)].add(terms.reshape(-1, BLOCK)), None)
    start = jnp.zeros((NX * NY, BLOCK), jnp.float32)
    summed, leftover = lax.scan(add_group, start, (block_ids.reshape(groups, RAYS_DEV, K), kernels.reshape(groups, RAYS_DEV, K, BLOCK), ray_weights.reshape(groups, RAYS_DEV)))
    return summed.reshape(NX, NY, BLOCK)

def reference(kernels, block_ids, delays):
    beta_now = jnp.sqrt(jnp.sum(delays * delays) + norm_epsilon)
    ray_part = delays / beta_now
    model_part = jnp.zeros((NX, NY, BLOCK), jnp.float32)
    direction = ray_transpose(ray_part, block_ids, kernels)
    alpha_now = jnp.sqrt(jnp.sum(direction * direction) + norm_epsilon)
    direction = direction / alpha_now
    search = direction
    solution = jnp.zeros((NX, NY, BLOCK), jnp.float32)
    phi_bar = beta_now
    rho_bar = alpha_now
    for iteration in range(ITERS):
        ray_part = ray_apply(direction, block_ids, kernels) - alpha_now * ray_part
        model_part = damping * laplace_grid(direction) - alpha_now * model_part
        beta_now = jnp.sqrt(jnp.sum(ray_part * ray_part) + jnp.sum(model_part * model_part) + norm_epsilon)
        ray_part = ray_part / beta_now
        model_part = model_part / beta_now
        rho_now = jnp.sqrt(rho_bar * rho_bar + beta_now * beta_now)
        cosine = rho_bar / rho_now
        sine_part = beta_now / rho_now
        phi_now = cosine * phi_bar
        phi_bar = sine_part * phi_bar
        solution = solution + phi_now / rho_now * search
        if iteration + 1 < ITERS:
            direction = ray_transpose(ray_part, block_ids, kernels) + damping * laplace_grid(model_part) - beta_now * direction
            alpha_now = jnp.sqrt(jnp.sum(direction * direction) + norm_epsilon)
            direction = direction / alpha_now
            theta_now = sine_part * alpha_now
            rho_bar = -cosine * alpha_now
            search = direction - theta_now / rho_now * search
    return solution
```

```python
import jax
import jax.numpy as jnp
from jax import lax
from jax.experimental import pallas as pl
from jax.experimental.pallas import tpu as pltpu
from jax.sharding import Mesh, PartitionSpec as P

CX = 8
NY = 128
damping = 0.3
norm_epsilon = 1e-06

F32 = jnp.float32
BF16 = jnp.bfloat16
I32 = jnp.int32

ALL = ("ev", "sx", "sz", "sc")
SLAB = ("sx", "sz", "sc")
D1 = ("sx", "sc")
D2 = ("ev", "sz")

VM = pl.BlockSpec(memory_space=pltpu.VMEM)


def iota(shape, dim):
    return lax.broadcasted_iota(I32, shape, dim)


def split2(x):
    hi = x.astype(BF16)
    return hi, (x - hi.astype(F32)).astype(BF16)


def call(body, out_shapes, scratch=(), flops=1000000, nbytes=1000000):
    outs = [jax.ShapeDtypeStruct(s, d) for s, d in out_shapes]
    return pl.pallas_call(
        body,
        out_shape=outs,
        in_specs=None,
        out_specs=[VM] * len(outs),
        scratch_shapes=list(scratch),
        compiler_params=pltpu.CompilerParams(vmem_limit_bytes=40 << 20),
        cost_estimate=pl.CostEstimate(flops=flops, bytes_accessed=nbytes, transcendentals=0),
    )


def run(body, args, out_shapes, scratch=(), flops=1000000, nbytes=1000000):
    outs = [jax.ShapeDtypeStruct(s, d) for s, d in out_shapes]
    return pl.pallas_call(
        body,
        out_shape=outs,
        in_specs=[VM] * len(args),
        out_specs=[VM] * len(outs),
        scratch_shapes=list(scratch),
        compiler_params=pltpu.CompilerParams(vmem_limit_bytes=40 << 20),
        cost_estimate=pl.CostEstimate(flops=flops, bytes_accessed=nbytes, transcendentals=0),
    )(*args)


def prep_kernel(ids_ref, b_ref, k_ref, send_ref, oh_ref):
    ids = ids_ref[...]
    slab = lax.shift_right_logical(ids, 10)
    loc = ids & 1023
    s_f = (iota((64, 1024), 0) == slab).astype(F32)
    s_b = s_f.astype(BF16)
    ra, ca = iota((128, 256), 0), iota((128, 256), 1)
    upper = jnp.where((ra < ca) | (ca >= 128), 1.0, 0.0).astype(BF16)
    stacked = jnp.concatenate([s_b[:, 128 * i : 128 * i + 128] for i in range(8)], axis=0)
    counts = jnp.dot(stacked, upper, preferred_element_type=F32)
    offset = jnp.zeros((64, 128), F32)
    ranks = []
    for i in range(8):
        block = counts[64 * i : 64 * i + 64]
        ranks.append(
            jnp.sum(
                s_f[:, 128 * i : 128 * i + 128] * (block[:, :128] + offset), axis=0, keepdims=True
            )
        )
        offset = offset + block[:, 128:]
    rank = jnp.concatenate(ranks, axis=1)
    for m in range(4):
        for r in range(4):
            pick = jnp.where(rank == float(4 * r + m), 1.0, 0.0).astype(BF16)
            oh_ref[64 * (4 * m + r) : 64 * (4 * m + r) + 64, :] = s_b * pick
    k_hi, k_lo = split2(k_ref[...])
    both = jnp.dot(
        oh_ref[...], jnp.concatenate([k_hi, k_lo], axis=1), preferred_element_type=F32
    )
    perm = both[:, :128] + both[:, 128:]
    lane_block = lax.shift_right_logical(iota((64, 128), 1), 5)
    for r in range(4):
        rows = [perm[64 * (4 * m + r) : 64 * (4 * m + r) + 64] for m in range(4)]
        for e in range(4):
            value = None
            for m in range(4):
                d = (m - e) % 4
                moved = rows[m] if d == 0 else pltpu.roll(rows[m], 32 * d, axis=1)
                value = moved if value is None else jnp.where(lane_block == m, moved, value)
            send_ref[pl.ds(320 * e + r, 64, stride=5), :] = value
    loc_i = lax.shift_right_logical(loc, 7)
    group = lax.shift_right_logical(loc_i, 1).astype(F32)
    column = ((loc_i & 1) * 128 + (loc & 127)).astype(F32)
    ray = lax.shift_right_logical(iota((1, 1024), 1), 5).astype(F32)
    b = b_ref[...]
    b_hi, rest = b.astype(BF16), None
    rest = b - b_hi.astype(F32)
    b_mid, b_lo = split2(rest)
    values = [group.astype(BF16), column.astype(BF16), ray.astype(BF16), b_hi, b_mid, b_lo]
    left = jnp.concatenate([s_b * v for v in values], axis=0)
    slot = (iota((128, 1024), 0) & 15).astype(F32)
    right = jnp.where(slot == rank, 1.0, 0.0).astype(BF16)
    info = lax.dot_general(left, right, (((1,), (1,)), ((), ())), preferred_element_type=F32)
    lane16 = lax.shift_right_logical(iota((64, 128), 1), 4)
    b_info = info[192:256] + info[256:320] + info[320:384]
    merged = jnp.where(
        lane16 == 0,
        info[0:64],
        jnp.where(lane16 == 1, info[64:128], jnp.where(lane16 == 2, info[128:192], b_info)),
    )
    for e in range(4):
        send_ref[pl.ds(320 * e + 4, 64, stride=5), :] = merged


def scatter_rows(kt_ref, j_ref, inf_ref, l_ref, weight_rows):
    for t in range(16):
        cols = slice(256 * t, 256 * t + 256)
        w_hi, w_lo = split2(kt_ref[:, cols] * weight_rows[t])
        group = inf_ref[t : t + 1, :]
        for i in range(4):
            mask = jnp.where(group == float(i), 1.0, 0.0).astype(BF16)
            l_ref[32 * i : 32 * i + 32, cols] = w_hi * mask
            l_ref[128 + 32 * i : 160 + 32 * i, cols] = w_lo * mask
    acc = lax.dot_general(
        l_ref[...], j_ref[...], (((1,), (1,)), ((), ())), preferred_element_type=F32
    )
    return acc[:128] + acc[128:]


def to_cube(flat):
    return [
        flat[32 * (i // 2) : 32 * (i // 2) + 32, 128 * (i % 2) : 128 * (i % 2) + 128]
        for i in range(8)
    ]


def gather_rays(flat, kt_ref, j_ref, inf_ref, g_ref):
    parts = jnp.concatenate(split2(flat), axis=0)
    ray_index = iota((32, 256), 0).astype(F32)
    total = jnp.zeros((32, 256), F32)
    for t in range(16):
        cols = slice(256 * t, 256 * t + 256)
        picked = jnp.dot(parts, j_ref[:, cols], preferred_element_type=F32)
        group = inf_ref[t : t + 1, :]
        value = jnp.zeros((32, 256), F32)
        for i in range(4):
            both = picked[32 * i : 32 * i + 32] + picked[128 + 32 * i : 160 + 32 * i]
            value = jnp.where(group == float(i), both, value)
        entry = jnp.sum(kt_ref[:, cols] * value, axis=0, keepdims=True)
        total = total + jnp.where(inf_ref[32 + t : 33 + t, :] == ray_index, entry, 0.0)
    for a in range(4):
        for h in range(2):
            g_ref[2 * a + h] = total[8 * a : 8 * a + 8, 128 * h : 128 * h + 128]


def first_kernel(r_ref, d_ref, low_ref, high_ref, g_ref, kt_ref, j_ref, inf_ref, l_ref):
    inf_ref[...] = r_ref[pl.ds(4, 256, stride=5), :].T[:64]
    for r in range(4):
        block = r_ref[pl.ds(r, 256, stride=5), :].T
        for m in range(4):
            t = 4 * r + m
            kt_ref[:, 256 * t : 256 * t + 256] = block[32 * m : 32 * m + 32]
    row = iota((256, 256), 0).astype(F32)
    for t in range(16):
        hit = jnp.where(row == inf_ref[16 + t : 17 + t, :], 1.0, 0.0)
        j_ref[:, 256 * t : 256 * t + 256] = hit.astype(BF16)
    flat = scatter_rows(
        kt_ref, j_ref, inf_ref, l_ref, [inf_ref[48 + t : 49 + t, :] for t in range(16)]
    )
    cube = to_cube(flat)
    for i in range(8):
        d_ref[i] = cube[i]
    for i in range(2):
        low_ref[i] = cube[i]
        high_ref[i] = cube[6 + i]
    gather_rays(flat, kt_ref, j_ref, inf_ref, g_ref)


def lane_neighbours(x, axis):
    size = x.shape[axis]
    lane = lax.broadcasted_iota(I32, x.shape, axis)
    up = jnp.where(lane == 0, 0.0, pltpu.roll(x, 1, axis=axis))
    down = jnp.where(lane == size - 1, 0.0, pltpu.roll(x, size - 1, axis=axis))
    return up + down


def square_kernel(ev_ref, d_ref, low_ref, high_ref, before_ref, after_ref, out_ref, e_ref, f_ref):
    ev = ev_ref[0]
    has_low = jnp.where(ev > 0, 1.0, 0.0)
    has_high = jnp.where(ev < 3, 1.0, 0.0)
    for i in range(12):
        if i < 2:
            own = low_ref[i]
        elif i < 10:
            own = d_ref[i - 2]
        else:
            own = high_ref[i - 10]
        e_ref[i, 8:40] = own
    for i in range(1, 11):
        index = 9 if i == 1 else i - 2
        e_ref[i, 0:8] = before_ref[index, 24:32] * has_low
        e_ref[i, 40:48] = after_ref[index, 0:8] * has_high
    for i in (0, 11):
        e_ref[i, 0:8] = jnp.zeros((8, 128), F32)
        e_ref[i, 40:48] = jnp.zeros((8, 128), F32)
    radial = iota((48, 128), 0)
    inside = jnp.where(radial < 8, has_low, jnp.where(radial >= 40, has_high, 1.0))

    def laplace(ref, i):
        x = ref[i]
        radial_sum = pltpu.roll(x, 1, axis=0) + pltpu.roll(x, 47, axis=0)
        return 6.0 * x - (ref[i - 1] + ref[i + 1] + radial_sum + lane_neighbours(x, 1))

    for i in range(1, 11):
        f_ref[i] = laplace(e_ref, i) * inside
    for i in range(2, 10):
        out_ref[i - 2] = laplace(f_ref, i)[8:40]


def second_kernel(
    g0_ref, kt_ref, j_ref, inf_ref, d_ref, ll_ref,
    w_ref, low_ref, high_ref, g_ref, scal_ref, l_ref,
):
    rays = jnp.concatenate(
        [jnp.concatenate([g0_ref[2 * a], g0_ref[2 * a + 1]], axis=1) for a in range(4)], axis=0
    )
    ray_index = iota((32, 256), 0).astype(F32)
    weights = [
        jnp.sum(
            jnp.where(inf_ref[32 + t : 33 + t, :] == ray_index, rays, 0.0), axis=0, keepdims=True
        )
        for t in range(16)
    ]
    flat = scatter_rows(kt_ref, j_ref, inf_ref, l_ref, weights)
    cube = to_cube(flat)
    cube = [cube[i] + (damping * damping) * ll_ref[i] for i in range(8)]
    dd = jnp.zeros((32, 128), F32)
    dw = jnp.zeros((32, 128), F32)
    ww = jnp.zeros((32, 128), F32)
    for i in range(8):
        w_ref[i] = cube[i]
        d = d_ref[i]
        dd = dd + d * d
        dw = dw + d * cube[i]
        ww = ww + cube[i] * cube[i]
    low_ref[0] = cube[0]
    high_ref[0] = cube[7]
    scal_ref[0:1] = jnp.sum(dd, axis=0, keepdims=True)
    scal_ref[1:2] = jnp.sum(dw, axis=0, keepdims=True)
    scal_ref[2:3] = jnp.sum(ww, axis=0, keepdims=True)
    whole = jnp.concatenate(
        [jnp.concatenate([cube[2 * i], cube[2 * i + 1]], axis=1) for i in range(4)], axis=0
    )
    gather_rays(whole, kt_ref, j_ref, inf_ref, g_ref)


def norms_kernel(
    ev_ref, w_ref, low_ref, high_ref, before_ref, after_ref, scal_ref, delay_ref, part_ref,
    out_ref, e_ref,
):
    ev = ev_ref[0]
    has_low = jnp.where(ev > 0, 1.0, 0.0)
    has_high = jnp.where(ev < 3, 1.0, 0.0)
    square = jnp.zeros((32, 128), F32)
    for i in range(8):
        e_ref[8:40] = w_ref[i]
        e_ref[0:8] = before_ref[i, 24:32] * has_low
        e_ref[40:48] = after_ref[i, 0:8] * has_high
        x = w_ref[i]
        left = low_ref[0] if i == 0 else w_ref[i - 1]
        right = high_ref[0] if i == 7 else w_ref[i + 1]
        value = 6.0 * x - (
            left + right + e_ref[7:39] + e_ref[9:41] + lane_neighbours(x, 1)
        )
        square = square + value * value
    lane = iota((1, 128), 1)
    b = delay_ref[...]
    numbers = [
        jnp.sum(scal_ref[0:1], axis=1, keepdims=True),
        jnp.sum(scal_ref[1:2], axis=1, keepdims=True),
        jnp.sum(scal_ref[2:3], axis=1, keepdims=True),
        jnp.sum(b * b, axis=1, keepdims=True),
        jnp.sum(jnp.sum(square, axis=0, keepdims=True), axis=1, keepdims=True),
    ]
    row = jnp.zeros((1, 128), F32)
    for n, number in enumerate(numbers):
        row = jnp.where(lane == n, number, row)
    total = part_ref[0]
    for i in range(1, 8):
        total = total + part_ref[i]
    for p in range(32):
        out_ref[9 * p : 9 * p + 8] = total
        out_ref[9 * p + 8 : 9 * p + 9] = row


def ray_norm_kernel(x_ref, out_ref):
    total = x_ref[0:8]
    row = x_ref[8:9]
    for p in range(1, 32):
        total = total + x_ref[9 * p : 9 * p + 8]
        row = row + x_ref[9 * p + 8 : 9 * p + 9]
    norm = jnp.sum(jnp.sum(total * total, axis=0, keepdims=True), axis=1, keepdims=True)
    row = jnp.where(iota((1, 128), 1) == 5, norm, row)
    out_ref[...] = jnp.broadcast_to(row, (8, 128))


def final_kernel(
    ev_ref, scal_ref, d0_ref, d1_ref, d2_ref, d3_ref, w0_ref, w1_ref, w2_ref, w3_ref,
    out_ref, x_ref,
):
    sums = jnp.sum(scal_ref[...], axis=0, keepdims=True)
    lane = iota((1, 128), 1)

    def number(n):
        return jnp.sum(jnp.where(lane == n, sums, 0.0), axis=1, keepdims=True)

    dd, dw, ww, bb = number(0), number(1), number(2), number(3)
    aa = number(5) + (damping * damping) * number(4)
    eps = norm_epsilon
    beta0 = jnp.sqrt(bb + eps)
    alpha0 = jnp.sqrt(dd / (beta0 * beta0) + eps)
    sigma0 = 1.0 / (beta0 * alpha0)
    ratio0 = alpha0 / beta0
    square1 = sigma0 * sigma0 * dw - 2.0 * sigma0 * ratio0 * dd + ratio0 * ratio0 * bb
    beta1 = jnp.sqrt(jnp.maximum(square1, 0.0) + eps)
    rho1 = jnp.sqrt(alpha0 * alpha0 + beta1 * beta1)
    cosine1, sine1 = alpha0 / rho1, beta1 / rho1
    phi1 = cosine1 * beta0
    phi_bar1 = sine1 * beta0
    shift = alpha0 * alpha0 + beta1 * beta1
    error2 = jnp.maximum(ww - 2.0 * shift * dw + shift * shift * dd, 0.0)
    scale1 = sigma0 / beta1
    alpha1 = jnp.sqrt(scale1 * scale1 * error2 + eps)
    tau = scale1 / alpha1
    theta1 = sine1 * alpha1
    rho_bar1 = -cosine1 * alpha1
    c1 = tau
    c0 = -tau * shift - alpha1 * sigma0 / beta1
    cb = alpha1 * ratio0 / beta1
    square2 = (
        c1 * c1 * aa
        + 2.0 * c1 * c0 * ww
        + c0 * c0 * dw
        + cb * cb * bb
        + 2.0 * c1 * cb * dw
        + 2.0 * c0 * cb * dd
    )
    beta2 = jnp.sqrt(jnp.maximum(square2, 0.0) + eps)
    rho2 = jnp.sqrt(rho_bar1 * rho_bar1 + beta2 * beta2)
    cosine2 = rho_bar1 / rho2
    phi2 = cosine2 * phi_bar1
    step = phi2 / rho2
    k1 = step * tau
    k0 = phi1 / rho1 * sigma0 - step * (tau * shift + theta1 / rho1 * sigma0)
    ev = ev_ref[0]
    pairs = ((d0_ref, w0_ref), (d1_ref, w1_ref), (d2_ref, w2_ref), (d3_ref, w3_ref))
    for n, (d_ref, w_ref) in enumerate(pairs):
        owner = (ev - n) & 3
        for i in range(8):
            x_ref[i, pl.ds(pl.multiple_of(32 * owner, 32), 32), :] = k0 * d_ref[i] + k1 * w_ref[i]
    for i in range(8):
        out_ref[i] = x_ref[i].T


def exchange(x, axes):
    return lax.all_to_all(x, axes, split_axis=0, concat_axis=0, tiled=True)


def on_device(kernels, block_ids, delays):
    def ring(count, distance):
        return [(i, (i + distance) % count) for i in range(count)]

    def slab_shift(x, distance):
        return lax.ppermute(x, SLAB, ring(64, distance))

    def ev_shift(x, distance):
        return lax.ppermute(x, "ev", ring(4, distance))

    ev = lax.axis_index("ev").reshape(1)
    ev_spec = pl.BlockSpec(memory_space=pltpu.SMEM)

    def run_ev(body, args, out_shapes, scratch=()):
        outs = [jax.ShapeDtypeStruct(s, d) for s, d in out_shapes]
        return pl.pallas_call(
            body,
            out_shape=outs,
            in_specs=[ev_spec] + [VM] * len(args),
            out_specs=[VM] * len(outs),
            scratch_shapes=list(scratch),
            compiler_params=pltpu.CompilerParams(vmem_limit_bytes=40 << 20),
            cost_estimate=pl.CostEstimate(
                flops=1000000, bytes_accessed=1000000, transcendentals=0
            ),
        )(ev, *args)

    ids = block_ids.reshape(1, 1024)
    weights = jnp.repeat(delays, 32).reshape(1, 1024)
    (send,) = run(
        prep_kernel,
        (ids, weights, kernels.reshape(1024, 128)),
        [((1280, 128), F32)],
        [pltpu.VMEM((1024, 1024), BF16)],
    )
    received = exchange(send.reshape(256, 1, 640), ALL).reshape(1280, 128)

    cube = ((8, 32, 128), F32)
    d0, d_low, d_high, rays, kt, one_hot, info = run(
        first_kernel,
        (received,),
        [
            cube,
            ((2, 32, 128), F32),
            ((2, 32, 128), F32),
            ((8, 8, 128), F32),
            ((32, 4096), F32),
            ((256, 4096), BF16),
            ((64, 256), F32),
        ],
        [pltpu.VMEM((256, 4096), BF16)],
    )
    below = slab_shift(d_high, 1)
    above = slab_shift(d_low, -1)
    wide = jnp.concatenate([d0, above[:1], below[1:]], axis=0)
    d_1, d_2, d_3 = (ev_shift(wide, n) for n in (1, 2, 3))

    rays = exchange(rays, D1)
    rays = jnp.broadcast_to(jnp.sum(rays, axis=0)[None], (32, 8, 128))
    rays = exchange(rays, D2)
    rays = jnp.broadcast_to(jnp.sum(rays, axis=0)[None], (8, 8, 128))
    rays = exchange(rays, D1)

    (square,) = run_ev(
        square_kernel,
        (d0, below, above, d_1, d_3),
        [cube],
        [pltpu.VMEM((12, 48, 128), F32), pltpu.VMEM((12, 48, 128), F32)],
    )
    w1, w_low, w_high, rays1, scal = run(
        second_kernel,
        (rays, kt, one_hot, info, d0, square),
        [cube, ((1, 32, 128), F32), ((1, 32, 128), F32), ((8, 8, 128), F32), ((8, 128), F32)],
        [pltpu.VMEM((256, 4096), BF16)],
    )
    w_below = slab_shift(w_high, 1)
    w_above = slab_shift(w_low, -1)
    w_1, w_3, w_2 = (ev_shift(w1, n) for n in (1, 3, 2))
    rays1 = exchange(rays1, D1)
    (packed,) = run_ev(
        norms_kernel,
        (w1, w_below, w_above, w_1, w_3, scal, delays.reshape(1, 32), rays1),
        [((288, 128), F32)],
        [pltpu.VMEM((48, 128), F32)],
    )
    packed = exchange(packed.reshape(32, 1, 1152), D2).reshape(288, 128)
    (sums,) = run(ray_norm_kernel, (packed,), [((8, 128), F32)])
    sums = exchange(sums.reshape(8, 1, 128), D1).reshape(8, 128)
    (out,) = run_ev(
        final_kernel,
        (sums, d0, d_1, d_2, d_3, w1, w_1, w_2, w_3),
        [((8, 128, 128), F32)],
        [pltpu.VMEM((8, 128, 128), F32)],
    )
    return out


def solution(mesh):
    fine = Mesh(mesh.devices.reshape(4, 4, 8, 2), ALL)
    rays = P(ALL)
    return jax.shard_map(
        on_device, mesh=fine, in_specs=(rays, rays, rays), out_specs=P(SLAB), check_vma=False
    )
```

```python
import jax
import jax.numpy as jnp
from jax import lax
from jax.experimental import pallas as pl
from jax.experimental.pallas import tpu as pltpu
from jax.sharding import Mesh, PartitionSpec as P

damping = 0.3
norm_epsilon = 1e-06

F32 = jnp.float32
BF16 = jnp.bfloat16
I32 = jnp.int32

ALL = ("ev", "sx", "sz", "sc")
SLAB = ("sx", "sz", "sc")
D1 = ("sx", "sc")
D2 = ("ev", "sz")
NEAR = ("ev", "sc")
FAR = ("sx", "sz")

VM = pl.BlockSpec(memory_space=pltpu.VMEM)


def iota(shape, dim):
    return lax.broadcasted_iota(I32, shape, dim)


def split2(x):
    hi = x.astype(BF16)
    return hi, (x - hi.astype(F32)).astype(BF16)


def run(body, args, out_shapes, scratch=(), flops=1000000, nbytes=1000000):
    outs = [jax.ShapeDtypeStruct(s, d) for s, d in out_shapes]
    return pl.pallas_call(
        body,
        out_shape=outs,
        in_specs=[VM] * len(args),
        out_specs=[VM] * len(outs),
        scratch_shapes=list(scratch),
        compiler_params=pltpu.CompilerParams(vmem_limit_bytes=16 << 20),
        cost_estimate=pl.CostEstimate(flops=flops, bytes_accessed=nbytes, transcendentals=0),
    )(*args)


def prep_kernel(ids_hbm, b_hbm, k_hbm, send_ref, oh_ref, ids_ref, b_ref, k_ref, sem):
    ids_copy = pltpu.make_async_copy(ids_hbm, ids_ref, sem.at[0])
    b_copy = pltpu.make_async_copy(b_hbm, b_ref, sem.at[1])
    copy = pltpu.make_async_copy(k_hbm, k_ref, sem.at[2])
    ids_copy.start()
    b_copy.start()
    copy.start()
    entry = iota((32, 1024), 1)
    sub = iota((32, 1024), 0)
    spread_k = jnp.where((entry & 31) == sub, 1.0, 0.0).astype(BF16)
    spread_ray = jnp.where(lax.shift_right_logical(entry, 5) == sub, 1.0, 0.0)
    ids_copy.wait()
    b_copy.wait()
    ids2 = ids_ref[...]
    halves = jnp.concatenate(
        [lax.shift_right_logical(ids2, 8).astype(F32), (ids2 & 255).astype(F32)], axis=0
    )
    halves = jnp.dot(halves.astype(BF16), spread_k, preferred_element_type=F32)
    ids = jnp.sum((halves[:32] * 256.0 + halves[32:]) * spread_ray, axis=0, keepdims=True)
    ids = ids.astype(I32)
    b = b_ref[...]
    b_hi = b.astype(BF16)
    b_mid, b_lo = split2(b - b_hi.astype(F32))
    b_rows = jnp.concatenate([jnp.broadcast_to(v, (16, 32)) for v in (b_hi, b_mid, b_lo)], axis=0)
    b_rows = jnp.dot(b_rows, spread_ray.astype(BF16), preferred_element_type=F32).astype(BF16)
    slab = lax.shift_right_logical(ids, 10)
    loc = ids & 1023
    s_f = (iota((64, 1024), 0) == slab).astype(F32)
    s_b = s_f.astype(BF16)
    ra, ca = iota((128, 256), 0), iota((128, 256), 1)
    upper = jnp.where((ra < ca) | (ca >= 128), 1.0, 0.0).astype(BF16)
    stacked = jnp.concatenate([s_b[:, 128 * i : 128 * i + 128] for i in range(8)], axis=0)
    counts = jnp.dot(stacked, upper, preferred_element_type=F32)
    offset = jnp.zeros((64, 128), F32)
    ranks = []
    for i in range(8):
        block = counts[64 * i : 64 * i + 64]
        ranks.append(
            jnp.sum(
                s_f[:, 128 * i : 128 * i + 128] * (block[:, :128] + offset), axis=0, keepdims=True
            )
        )
        offset = offset + block[:, 128:]
    rank = jnp.concatenate(ranks, axis=1)
    for m in range(4):
        for r in range(4):
            pick = jnp.where(rank == float(4 * r + m), 1.0, 0.0).astype(BF16)
            oh_ref[64 * (4 * m + r) : 64 * (4 * m + r) + 64, :] = s_b * pick
    copy.wait()
    k_hi, k_lo = split2(k_ref[...])
    both = jnp.dot(
        oh_ref[...], jnp.concatenate([k_hi, k_lo], axis=1), preferred_element_type=F32
    )
    perm = both[:, :128] + both[:, 128:]
    lane_block = lax.shift_right_logical(iota((64, 128), 1), 5)
    for r in range(4):
        rows = [perm[64 * (4 * m + r) : 64 * (4 * m + r) + 64] for m in range(4)]
        for e in range(4):
            value = None
            for m in range(4):
                d = (m - e) % 4
                moved = rows[m] if d == 0 else pltpu.roll(rows[m], 32 * d, axis=1)
                value = moved if value is None else jnp.where(lane_block == m, moved, value)
            send_ref[pl.ds(320 * e + r, 64, stride=5), :] = value
    loc_i = lax.shift_right_logical(loc, 7)
    group = lax.shift_right_logical(loc_i, 1).astype(F32)
    column = ((loc_i & 1) * 128 + (loc & 127)).astype(F32)
    ray = lax.shift_right_logical(iota((1, 1024), 1), 5).astype(F32)
    b_parts = [b_rows[16 * i : 16 * i + 1] for i in range(3)]
    values = [group.astype(BF16), column.astype(BF16), ray.astype(BF16)] + b_parts
    left = jnp.concatenate([s_b * v for v in values], axis=0)
    slot = (iota((128, 1024), 0) & 15).astype(F32)
    right = jnp.where(slot == rank, 1.0, 0.0).astype(BF16)
    info = lax.dot_general(left, right, (((1,), (1,)), ((), ())), preferred_element_type=F32)
    lane16 = lax.shift_right_logical(iota((64, 128), 1), 4)
    b_info = info[192:256] + info[256:320] + info[320:384]
    merged = jnp.where(
        lane16 == 0,
        info[0:64],
        jnp.where(lane16 == 1, info[64:128], jnp.where(lane16 == 2, info[128:192], b_info)),
    )
    for e in range(4):
        send_ref[pl.ds(320 * e + 4, 64, stride=5), :] = merged


def scatter_rows(kt_ref, j_ref, inf_ref, l_ref, weight_rows):
    for t in range(16):
        cols = slice(256 * t, 256 * t + 256)
        w_hi, w_lo = split2(kt_ref[:, cols] * weight_rows[t])
        group = inf_ref[t : t + 1, :]
        for i in range(4):
            mask = jnp.where(group == float(i), 1.0, 0.0).astype(BF16)
            l_ref[32 * i : 32 * i + 32, cols] = w_hi * mask
            l_ref[128 + 32 * i : 160 + 32 * i, cols] = w_lo * mask
    acc = lax.dot_general(
        l_ref[...], j_ref[...], (((1,), (1,)), ((), ())), preferred_element_type=F32
    )
    return acc[:128] + acc[128:]


def to_cube(flat):
    return [
        flat[32 * (i // 2) : 32 * (i // 2) + 32, 128 * (i % 2) : 128 * (i % 2) + 128]
        for i in range(8)
    ]


def gather_rays(flat, kt_ref, j_ref, inf_ref, g_ref):
    parts = jnp.concatenate(split2(flat), axis=0)
    ray_index = iota((32, 256), 0).astype(F32)
    total = jnp.zeros((32, 256), F32)
    for t in range(16):
        cols = slice(256 * t, 256 * t + 256)
        picked = jnp.dot(parts, j_ref[:, cols], preferred_element_type=F32)
        group = inf_ref[t : t + 1, :]
        value = jnp.zeros((32, 256), F32)
        for i in range(4):
            both = picked[32 * i : 32 * i + 32] + picked[128 + 32 * i : 160 + 32 * i]
            value = jnp.where(group == float(i), both, value)
        entry = jnp.sum(kt_ref[:, cols] * value, axis=0, keepdims=True)
        total = total + jnp.where(inf_ref[32 + t : 33 + t, :] == ray_index, entry, 0.0)
    for a in range(4):
        for h in range(2):
            g_ref[2 * a + h, 0:8] = total[8 * a : 8 * a + 8, 128 * h : 128 * h + 128]


def first_kernel(r_ref, d_ref, low_ref, high_ref, g_ref, kt_ref, j_ref, inf_ref, l_ref):
    inf_ref[...] = r_ref[pl.ds(4, 256, stride=5), :].T[:64]
    for r in range(4):
        block = r_ref[pl.ds(r, 256, stride=5), :].T
        for m in range(4):
            t = 4 * r + m
            kt_ref[:, 256 * t : 256 * t + 256] = block[32 * m : 32 * m + 32]
    row = iota((256, 256), 0).astype(F32)
    for t in range(16):
        hit = jnp.where(row == inf_ref[16 + t : 17 + t, :], 1.0, 0.0)
        j_ref[:, 256 * t : 256 * t + 256] = hit.astype(BF16)
    flat = scatter_rows(
        kt_ref, j_ref, inf_ref, l_ref, [inf_ref[48 + t : 49 + t, :] for t in range(16)]
    )
    cube = to_cube(flat)
    for i in range(8):
        d_ref[i] = cube[i]
    for i in range(2):
        low_ref[i] = cube[i]
        high_ref[i] = cube[6 + i]
    gather_rays(flat, kt_ref, j_ref, inf_ref, g_ref)


def lane_neighbours(x, axis):
    size = x.shape[axis]
    lane = lax.broadcasted_iota(I32, x.shape, axis)
    up = jnp.where(lane == 0, 0.0, pltpu.roll(x, 1, axis=axis))
    down = jnp.where(lane == size - 1, 0.0, pltpu.roll(x, size - 1, axis=axis))
    return up + down


def apply_square(ev, d_ref, low_ref, high_ref, before_ref, after_ref, e_ref, f_ref):
    has_low = jnp.where(ev > 0, 1.0, 0.0)
    has_high = jnp.where(ev < 3, 1.0, 0.0)
    for i in range(12):
        if i < 2:
            own = low_ref[i]
        elif i < 10:
            own = d_ref[i - 2]
        else:
            own = high_ref[i - 10]
        e_ref[i, 8:40] = own
    for i in range(1, 11):
        index = 9 if i == 1 else i - 2
        e_ref[i, 0:8] = before_ref[index, 24:32] * has_low
        e_ref[i, 40:48] = after_ref[index, 0:8] * has_high
    for i in (0, 11):
        e_ref[i, 0:8] = jnp.zeros((8, 128), F32)
        e_ref[i, 40:48] = jnp.zeros((8, 128), F32)
    radial = iota((48, 128), 0)
    inside = jnp.where(radial < 8, has_low, jnp.where(radial >= 40, has_high, 1.0))

    def laplace(ref, i):
        x = ref[i]
        radial_sum = pltpu.roll(x, 1, axis=0) + pltpu.roll(x, 47, axis=0)
        return 6.0 * x - (ref[i - 1] + ref[i + 1] + radial_sum + lane_neighbours(x, 1))

    for i in range(1, 11):
        f_ref[i] = laplace(e_ref, i) * inside
    return [laplace(f_ref, i)[8:40] for i in range(2, 10)]


def second_kernel(
    place_ref, g0_ref, kt_ref, j_ref, inf_ref, d_ref, below_ref, above_ref, before_ref, after_ref,
    w_ref, edge_ref, near_ref, g_ref, scal_ref, l_ref, e_ref, f_ref,
):
    ev = lax.shift_right_logical(place_ref[0], 6)
    core = place_ref[0] & 1
    rays = jnp.concatenate(
        [jnp.concatenate([g0_ref[2 * a], g0_ref[2 * a + 1]], axis=1) for a in range(4)], axis=0
    )
    ray_index = iota((32, 256), 0).astype(F32)
    weights = [
        jnp.sum(
            jnp.where(inf_ref[32 + t : 33 + t, :] == ray_index, rays, 0.0), axis=0, keepdims=True
        )
        for t in range(16)
    ]
    flat = scatter_rows(kt_ref, j_ref, inf_ref, l_ref, weights)
    cube = to_cube(flat)
    square = apply_square(ev, d_ref, below_ref, above_ref, before_ref, after_ref, e_ref, f_ref)
    cube = [cube[i] + (damping * damping) * square[i] for i in range(8)]
    dd = jnp.zeros((32, 128), F32)
    dw = jnp.zeros((32, 128), F32)
    ww = jnp.zeros((32, 128), F32)
    for i in range(8):
        w_ref[i] = cube[i]
        d = d_ref[i]
        dd = dd + d * d
        dw = dw + d * cube[i]
        ww = ww + cube[i] * cube[i]
    even = jnp.where(core == 0, 1.0, 0.0)
    edge_ref[0] = even * cube[0] + (1.0 - even) * cube[7]
    near_ref[0] = even * cube[7] + (1.0 - even) * cube[0]
    first = jnp.concatenate([cube[i][0:1] for i in range(8)], axis=0)
    last = jnp.concatenate([cube[i][31:32] for i in range(8)], axis=0)
    g_ref[2 * ((ev + 1) & 3) + core, 8:16] = last
    g_ref[2 * ((ev + 3) & 3) + core, 8:16] = first
    scal_ref[0:1] = jnp.sum(dd, axis=0, keepdims=True)
    scal_ref[1:2] = jnp.sum(dw, axis=0, keepdims=True)
    scal_ref[2:3] = jnp.sum(ww, axis=0, keepdims=True)
    whole = jnp.concatenate(
        [jnp.concatenate([cube[2 * i], cube[2 * i + 1]], axis=1) for i in range(4)], axis=0
    )
    gather_rays(whole, kt_ref, j_ref, inf_ref, g_ref)


def norms_kernel(place_ref, w_ref, edge_ref, near_ref, scal_ref, delay_ref, part_ref, out_ref, e_ref):
    ev = lax.shift_right_logical(place_ref[0], 6)
    core = place_ref[0] & 1
    even = jnp.where(core == 0, 1.0, 0.0)
    has_low = jnp.where(ev > 0, 1.0, 0.0)
    has_high = jnp.where(ev < 3, 1.0, 0.0)
    partner = near_ref[0]
    far = edge_ref[0]
    low = even * far + (1.0 - even) * partner
    high = even * partner + (1.0 - even) * far
    before = part_ref[2 * ((ev + 3) & 3) + core, 8:16] * has_low
    after = part_ref[2 * ((ev + 1) & 3) + core, 8:16] * has_high
    square = jnp.zeros((32, 128), F32)
    for i in range(8):
        x = w_ref[i]
        e_ref[8:40] = x
        e_ref[7:8] = before[i : i + 1]
        e_ref[40:41] = after[i : i + 1]
        left = low if i == 0 else w_ref[i - 1]
        right = high if i == 7 else w_ref[i + 1]
        value = 6.0 * x - (
            left + right + e_ref[7:39] + e_ref[9:41] + lane_neighbours(x, 1)
        )
        square = square + value * value
    lane = iota((1, 128), 1)
    b = delay_ref[...]
    numbers = [
        jnp.sum(scal_ref[0:1], axis=1, keepdims=True),
        jnp.sum(scal_ref[1:2], axis=1, keepdims=True),
        jnp.sum(scal_ref[2:3], axis=1, keepdims=True),
        jnp.sum(b * b, axis=1, keepdims=True),
        jnp.sum(jnp.sum(square, axis=0, keepdims=True), axis=1, keepdims=True),
    ]
    row = jnp.zeros((1, 128), F32)
    for n, number in enumerate(numbers):
        row = jnp.where(lane == n, number, row)
    total = part_ref[0, 0:8]
    for i in range(1, 8):
        total = total + part_ref[i, 0:8]
    for p in range(32):
        out_ref[9 * p : 9 * p + 8] = total
        out_ref[9 * p + 8 : 9 * p + 9] = row


def spread_kernel(x_ref, out_ref):
    total = x_ref[0]
    for i in range(1, x_ref.shape[0]):
        total = total + x_ref[i]
    for i in range(out_ref.shape[0]):
        out_ref[i] = total


def ray_norm_kernel(x_ref, out_ref):
    total = x_ref[0:8]
    row = x_ref[8:9]
    for p in range(1, 32):
        total = total + x_ref[9 * p : 9 * p + 8]
        row = row + x_ref[9 * p + 8 : 9 * p + 9]
    norm = jnp.sum(jnp.sum(total * total, axis=0, keepdims=True), axis=1, keepdims=True)
    row = jnp.where(iota((1, 128), 1) == 5, norm, row)
    out_ref[...] = jnp.broadcast_to(row, (8, 128))


def final_kernel(
    place_ref, scal_ref, d0_ref, d1_ref, d2_ref, d3_ref, w0_ref, w1_ref, w2_ref, w3_ref,
    out_ref, x_ref,
):
    sums = jnp.sum(scal_ref[...], axis=0, keepdims=True)
    lane = iota((1, 128), 1)

    def number(n):
        return jnp.sum(jnp.where(lane == n, sums, 0.0), axis=1, keepdims=True)

    dd, dw, ww, bb = number(0), number(1), number(2), number(3)
    aa = number(5) + (damping * damping) * number(4)
    eps = norm_epsilon
    beta0 = jnp.sqrt(bb + eps)
    alpha0 = jnp.sqrt(dd / (beta0 * beta0) + eps)
    sigma0 = 1.0 / (beta0 * alpha0)
    ratio0 = alpha0 / beta0
    square1 = sigma0 * sigma0 * dw - 2.0 * sigma0 * ratio0 * dd + ratio0 * ratio0 * bb
    beta1 = jnp.sqrt(jnp.maximum(square1, 0.0) + eps)
    rho1 = jnp.sqrt(alpha0 * alpha0 + beta1 * beta1)
    cosine1, sine1 = alpha0 / rho1, beta1 / rho1
    phi1 = cosine1 * beta0
    phi_bar1 = sine1 * beta0
    shift = alpha0 * alpha0 + beta1 * beta1
    error2 = jnp.maximum(ww - 2.0 * shift * dw + shift * shift * dd, 0.0)
    scale1 = sigma0 / beta1
    alpha1 = jnp.sqrt(scale1 * scale1 * error2 + eps)
    tau = scale1 / alpha1
    theta1 = sine1 * alpha1
    rho_bar1 = -cosine1 * alpha1
    c1 = tau
    c0 = -tau * shift - alpha1 * sigma0 / beta1
    cb = alpha1 * ratio0 / beta1
    square2 = (
        c1 * c1 * aa
        + 2.0 * c1 * c0 * ww
        + c0 * c0 * dw
        + cb * cb * bb
        + 2.0 * c1 * cb * dw
        + 2.0 * c0 * cb * dd
    )
    beta2 = jnp.sqrt(jnp.maximum(square2, 0.0) + eps)
    rho2 = jnp.sqrt(rho_bar1 * rho_bar1 + beta2 * beta2)
    cosine2 = rho_bar1 / rho2
    phi2 = cosine2 * phi_bar1
    step = phi2 / rho2
    k1 = step * tau
    k0 = phi1 / rho1 * sigma0 - step * (tau * shift + theta1 / rho1 * sigma0)
    ev = lax.shift_right_logical(place_ref[0], 6)
    pairs = ((d0_ref, w0_ref), (d1_ref, w1_ref), (d2_ref, w2_ref), (d3_ref, w3_ref))
    for n, (d_ref, w_ref) in enumerate(pairs):
        owner = (ev - n) & 3
        for i in range(8):
            x_ref[i, pl.ds(pl.multiple_of(32 * owner, 32), 32), :] = k0 * d_ref[i] + k1 * w_ref[i]
    for i in range(8):
        out_ref[i] = x_ref[i].T


def exchange(x, axes):
    return lax.all_to_all(x, axes, split_axis=0, concat_axis=0, tiled=True)


def body(kernels, block_ids, delays):
    def ring(count, distance):
        return [(i, (i + distance) % count) for i in range(count)]

    def slab_shift(x, distance):
        return lax.ppermute(x, SLAB, ring(64, distance))

    def ev_shift(x, distance):
        return lax.ppermute(x, "ev", ring(4, distance))

    place = lax.axis_index(ALL).reshape(1)
    ev_spec = pl.BlockSpec(memory_space=pltpu.SMEM)

    def run_ev(body, args, out_shapes, scratch=()):
        outs = [jax.ShapeDtypeStruct(s, d) for s, d in out_shapes]
        return pl.pallas_call(
            body,
            out_shape=outs,
            in_specs=[ev_spec] + [VM] * len(args),
            out_specs=[VM] * len(outs),
            scratch_shapes=list(scratch),
            compiler_params=pltpu.CompilerParams(vmem_limit_bytes=16 << 20),
            cost_estimate=pl.CostEstimate(
                flops=1000000, bytes_accessed=1000000, transcendentals=0
            ),
        )(place, *args)

    send = pl.pallas_call(
        prep_kernel,
        out_shape=jax.ShapeDtypeStruct((1280, 128), F32),
        in_specs=[pl.BlockSpec(memory_space=pltpu.MemorySpace.HBM)] * 3,
        out_specs=VM,
        scratch_shapes=[
            pltpu.VMEM((1024, 1024), BF16),
            pltpu.VMEM((32, 32), I32),
            pltpu.VMEM((1, 32), F32),
            pltpu.VMEM((1024, 128), F32),
            pltpu.SemaphoreType.DMA((3,)),
        ],
        compiler_params=pltpu.CompilerParams(vmem_limit_bytes=63 << 20),
    )(block_ids, delays.reshape(1, 32), kernels.reshape(1024, 128))
    received = exchange(send.reshape(256, 1, 640), ALL).reshape(1280, 128)

    cube = ((8, 32, 128), F32)
    d0, d_low, d_high, rays, kt, one_hot, info = run(
        first_kernel,
        (received,),
        [
            cube,
            ((2, 32, 128), F32),
            ((2, 32, 128), F32),
            ((8, 8, 128), F32),
            ((32, 4096), F32),
            ((256, 4096), BF16),
            ((64, 256), F32),
        ],
        [pltpu.VMEM((256, 4096), BF16)],
    )
    below = slab_shift(d_high, 1)
    above = slab_shift(d_low, -1)
    wide = jnp.concatenate([d0, above[:1], below[1:]], axis=0)
    d_1, d_2, d_3 = (ev_shift(wide, n) for n in (1, 2, 3))

    rays = exchange(rays, D1)
    (rays,) = run(spread_kernel, (rays,), [((32, 8, 128), F32)])
    rays = exchange(rays, D2)
    (rays,) = run(spread_kernel, (rays,), [((8, 8, 128), F32)])
    rays = exchange(rays, D1)

    w1, w_edge, w_near, rays1, scal = run_ev(
        second_kernel,
        (rays, kt, one_hot, info, d0, below, above, d_1, d_3),
        [cube, ((1, 32, 128), F32), ((1, 32, 128), F32), ((8, 16, 128), F32), ((8, 128), F32)],
        [
            pltpu.VMEM((256, 4096), BF16),
            pltpu.VMEM((12, 48, 128), F32),
            pltpu.VMEM((12, 48, 128), F32),
        ],
    )
    pairs = [(i, (i + 1) % 64 if i % 2 else (i - 1) % 64) for i in range(64)]
    w_far = lax.ppermute(w_edge, SLAB, pairs)
    w_near = lax.ppermute(w_near, "sc", [(0, 1), (1, 0)])
    rays1 = exchange(rays1, NEAR)
    (packed,) = run_ev(
        norms_kernel,
        (w1, w_far, w_near, scal, delays.reshape(1, 32), rays1),
        [((288, 128), F32)],
        [pltpu.VMEM((48, 128), F32)],
    )
    w_1, w_2, w_3 = (ev_shift(w1, n) for n in (1, 2, 3))
    packed = exchange(packed.reshape(32, 1, 1152), FAR).reshape(288, 128)
    packed, d_2, w_1, w_2, w_3 = lax.optimization_barrier((packed, d_2, w_1, w_2, w_3))
    (sums,) = run(ray_norm_kernel, (packed,), [((8, 128), F32)])
    sums = exchange(sums.reshape(8, 1, 128), NEAR).reshape(8, 128)
    (out,) = run_ev(
        final_kernel,
        (sums, d0, d_1, d_2, d_3, w1, w_1, w_2, w_3),
        [((8, 128, 128), F32)],
        [pltpu.VMEM((8, 128, 128), F32)],
    )
    return out


def solution(mesh):
    fine = Mesh(mesh.devices.reshape(4, 4, 8, 2), ALL)
    rays = P(ALL)
    return jax.shard_map(
        body, mesh=fine, in_specs=(rays, rays, rays), out_specs=P(SLAB), check_vma=False
    )
```

```python
import jax
import jax.numpy as jnp
from jax import lax
from jax.experimental import pallas as pl
from jax.experimental.pallas import tpu as pltpu
from jax.sharding import Mesh, PartitionSpec as P

damping = 0.3
norm_epsilon = 1e-06

F32 = jnp.float32
BF16 = jnp.bfloat16
I32 = jnp.int32


ALL = ("ev", "sx", "sz", "sc")
SLAB = ("sx", "sz", "sc")
D1 = ("sx", "sc")
D2 = ("ev", "sz")
NEAR = ("ev", "sc")
FAR = ("sx", "sz")

VM = pl.BlockSpec(memory_space=pltpu.VMEM)


def iota(shape, dim):
    return lax.broadcasted_iota(I32, shape, dim)


def split2(x):
    hi = x.astype(BF16)
    return hi, (x - hi.astype(F32)).astype(BF16)


def run(body, args, out_shapes, scratch=(), flops=1000000, nbytes=1000000):
    outs = [jax.ShapeDtypeStruct(s, d) for s, d in out_shapes]
    return pl.pallas_call(
        body,
        out_shape=outs,
        in_specs=[VM] * len(args),
        out_specs=[VM] * len(outs),
        scratch_shapes=list(scratch),
        compiler_params=pltpu.CompilerParams(vmem_limit_bytes=16 << 20),
        cost_estimate=pl.CostEstimate(flops=flops, bytes_accessed=nbytes, transcendentals=0),
    )(*args)


def prep_kernel(ids_hbm, b_hbm, k_hbm, send_ref, oh_ref, ids_ref, b_ref, k_ref, sem):
    ids_copy = pltpu.make_async_copy(ids_hbm, ids_ref, sem.at[0])
    b_copy = pltpu.make_async_copy(b_hbm, b_ref, sem.at[1])
    copy = pltpu.make_async_copy(k_hbm, k_ref, sem.at[2])
    ids_copy.start()
    b_copy.start()
    copy.start()
    entry = iota((32, 1024), 1)
    sub = iota((32, 1024), 0)
    spread_k = jnp.where((entry & 31) == sub, 1.0, 0.0).astype(BF16)
    spread_ray = jnp.where(lax.shift_right_logical(entry, 5) == sub, 1.0, 0.0)
    ids_copy.wait()
    b_copy.wait()
    ids2 = ids_ref[...]
    halves = jnp.concatenate(
        [lax.shift_right_logical(ids2, 8).astype(F32), (ids2 & 255).astype(F32)], axis=0
    )
    halves = jnp.dot(halves.astype(BF16), spread_k, preferred_element_type=F32)
    ids = jnp.sum((halves[:32] * 256.0 + halves[32:]) * spread_ray, axis=0, keepdims=True)
    ids = ids.astype(I32)
    b = b_ref[...]
    b_hi = b.astype(BF16)
    b_mid, b_lo = split2(b - b_hi.astype(F32))
    b_rows = jnp.concatenate([jnp.broadcast_to(v, (16, 32)) for v in (b_hi, b_mid, b_lo)], axis=0)
    b_rows = jnp.dot(b_rows, spread_ray.astype(BF16), preferred_element_type=F32).astype(BF16)
    slab = lax.shift_right_logical(ids, 10)
    loc = ids & 1023
    s_f = (iota((64, 1024), 0) == slab).astype(F32)
    s_b = s_f.astype(BF16)
    ra, ca = iota((128, 256), 0), iota((128, 256), 1)
    upper = jnp.where((ra < ca) | (ca >= 128), 1.0, 0.0).astype(BF16)
    stacked = jnp.concatenate([s_b[:, 128 * i : 128 * i + 128] for i in range(8)], axis=0)
    counts = jnp.dot(stacked, upper, preferred_element_type=F32)
    offset = jnp.zeros((64, 128), F32)
    ranks = []
    for i in range(8):
        block = counts[64 * i : 64 * i + 64]
        ranks.append(
            jnp.sum(
                s_f[:, 128 * i : 128 * i + 128] * (block[:, :128] + offset), axis=0, keepdims=True
            )
        )
        offset = offset + block[:, 128:]
    rank = jnp.concatenate(ranks, axis=1)
    for m in range(4):
        for r in range(4):
            pick = jnp.where(rank == float(4 * r + m), 1.0, 0.0).astype(BF16)
            oh_ref[64 * (4 * m + r) : 64 * (4 * m + r) + 64, :] = s_b * pick
    copy.wait()
    k_hi, k_lo = split2(k_ref[...])
    both = jnp.dot(
        oh_ref[...], jnp.concatenate([k_hi, k_lo], axis=1), preferred_element_type=F32
    )
    perm = both[:, :128] + both[:, 128:]
    lane_block = lax.shift_right_logical(iota((64, 128), 1), 5)
    for r in range(4):
        rows = [perm[64 * (4 * m + r) : 64 * (4 * m + r) + 64] for m in range(4)]
        for e in range(4):
            value = None
            for m in range(4):
                d = (m - e) % 4
                moved = rows[m] if d == 0 else pltpu.roll(rows[m], 32 * d, axis=1)
                value = moved if value is None else jnp.where(lane_block == m, moved, value)
            send_ref[pl.ds(320 * e + r, 64, stride=5), :] = value
    loc_i = lax.shift_right_logical(loc, 7)
    group = lax.shift_right_logical(loc_i, 1).astype(F32)
    column = ((loc_i & 1) * 128 + (loc & 127)).astype(F32)
    ray = lax.shift_right_logical(iota((1, 1024), 1), 5).astype(F32)
    b_parts = [b_rows[16 * i : 16 * i + 1] for i in range(3)]
    values = [group.astype(BF16), column.astype(BF16), ray.astype(BF16)] + b_parts
    left = jnp.concatenate([s_b * v for v in values], axis=0)
    slot = (iota((128, 1024), 0) & 15).astype(F32)
    right = jnp.where(slot == rank, 1.0, 0.0).astype(BF16)
    info = lax.dot_general(left, right, (((1,), (1,)), ((), ())), preferred_element_type=F32)
    lane16 = lax.shift_right_logical(iota((64, 128), 1), 4)
    b_info = info[192:256] + info[256:320] + info[320:384]
    merged = jnp.where(
        lane16 == 0,
        info[0:64],
        jnp.where(lane16 == 1, info[64:128], jnp.where(lane16 == 2, info[128:192], b_info)),
    )
    for e in range(4):
        send_ref[pl.ds(320 * e + 4, 64, stride=5), :] = merged


def scatter_rows(kt_ref, j_ref, inf_ref, l_ref, weight_rows):
    for t in range(16):
        cols = slice(256 * t, 256 * t + 256)
        w_hi, w_lo = split2(kt_ref[:, cols] * weight_rows[t])
        group = inf_ref[t : t + 1, :]
        for i in range(4):
            mask = jnp.where(group == float(i), 1.0, 0.0).astype(BF16)
            l_ref[32 * i : 32 * i + 32, cols] = w_hi * mask
            l_ref[128 + 32 * i : 160 + 32 * i, cols] = w_lo * mask
    acc = lax.dot_general(
        l_ref[...], j_ref[...], (((1,), (1,)), ((), ())), preferred_element_type=F32
    )
    return acc[:128] + acc[128:]


def to_cube(flat):
    return [
        flat[32 * (i // 2) : 32 * (i // 2) + 32, 128 * (i % 2) : 128 * (i % 2) + 128]
        for i in range(8)
    ]


def gather_rays(flat, kt_ref, j_ref, inf_ref, g_ref):
    parts = jnp.concatenate(split2(flat), axis=0)
    ray_index = iota((32, 256), 0).astype(F32)
    total = jnp.zeros((32, 256), F32)
    for t in range(16):
        cols = slice(256 * t, 256 * t + 256)
        picked = jnp.dot(parts, j_ref[:, cols], preferred_element_type=F32)
        group = inf_ref[t : t + 1, :]
        value = jnp.zeros((32, 256), F32)
        for i in range(4):
            both = picked[32 * i : 32 * i + 32] + picked[128 + 32 * i : 160 + 32 * i]
            value = jnp.where(group == float(i), both, value)
        entry = jnp.sum(kt_ref[:, cols] * value, axis=0, keepdims=True)
        total = total + jnp.where(inf_ref[32 + t : 33 + t, :] == ray_index, entry, 0.0)
    for a in range(4):
        for h in range(2):
            g_ref[2 * a + h, 0:8] = total[8 * a : 8 * a + 8, 128 * h : 128 * h + 128]


def first_kernel(r_ref, d_ref, low_ref, high_ref, g_ref, kt_ref, j_ref, inf_ref, l_ref):
    inf_ref[...] = r_ref[pl.ds(4, 256, stride=5), :].T[:64]
    for r in range(4):
        block = r_ref[pl.ds(r, 256, stride=5), :].T
        for m in range(4):
            t = 4 * r + m
            kt_ref[:, 256 * t : 256 * t + 256] = block[32 * m : 32 * m + 32]
    row = iota((256, 256), 0).astype(F32)
    for t in range(16):
        hit = jnp.where(row == inf_ref[16 + t : 17 + t, :], 1.0, 0.0)
        j_ref[:, 256 * t : 256 * t + 256] = hit.astype(BF16)
    flat = scatter_rows(
        kt_ref, j_ref, inf_ref, l_ref, [inf_ref[48 + t : 49 + t, :] for t in range(16)]
    )
    cube = to_cube(flat)
    for i in range(8):
        d_ref[i] = cube[i]
    for i in range(2):
        low_ref[i] = cube[i]
        high_ref[i] = cube[6 + i]
    gather_rays(flat, kt_ref, j_ref, inf_ref, g_ref)


def lane_neighbours(x, axis):
    size = x.shape[axis]
    lane = lax.broadcasted_iota(I32, x.shape, axis)
    up = jnp.where(lane == 0, 0.0, pltpu.roll(x, 1, axis=axis))
    down = jnp.where(lane == size - 1, 0.0, pltpu.roll(x, size - 1, axis=axis))
    return up + down


def apply_square(ev, d_ref, low_ref, high_ref, before_ref, after_ref, e_ref, f_ref):
    has_low = jnp.where(ev > 0, 1.0, 0.0)
    has_high = jnp.where(ev < 3, 1.0, 0.0)
    for i in range(12):
        if i < 2:
            own = low_ref[i]
        elif i < 10:
            own = d_ref[i - 2]
        else:
            own = high_ref[i - 10]
        e_ref[i, 8:40] = own
    for i in range(1, 11):
        index = 9 if i == 1 else i - 2
        e_ref[i, 0:8] = before_ref[index, 24:32] * has_low
        e_ref[i, 40:48] = after_ref[index, 0:8] * has_high
    for i in (0, 11):
        e_ref[i, 0:8] = jnp.zeros((8, 128), F32)
        e_ref[i, 40:48] = jnp.zeros((8, 128), F32)
    radial = iota((48, 128), 0)
    inside = jnp.where(radial < 8, has_low, jnp.where(radial >= 40, has_high, 1.0))

    def laplace(ref, i):
        x = ref[i]
        radial_sum = pltpu.roll(x, 1, axis=0) + pltpu.roll(x, 47, axis=0)
        return 6.0 * x - (ref[i - 1] + ref[i + 1] + radial_sum + lane_neighbours(x, 1))

    for i in range(1, 11):
        f_ref[i] = laplace(e_ref, i) * inside
    return [laplace(f_ref, i)[8:40] for i in range(2, 10)]


def apply_kernel(g0_ref, kt_ref, j_ref, inf_ref, t_ref, l_ref):
    rays = jnp.concatenate(
        [jnp.concatenate([g0_ref[2 * a], g0_ref[2 * a + 1]], axis=1) for a in range(4)], axis=0
    )
    ray_index = iota((32, 256), 0).astype(F32)
    weights = [
        jnp.sum(
            jnp.where(inf_ref[32 + t : 33 + t, :] == ray_index, rays, 0.0), axis=0, keepdims=True
        )
        for t in range(16)
    ]
    t_ref[...] = scatter_rows(kt_ref, j_ref, inf_ref, l_ref, weights)


def second_kernel(
    place_ref, t_ref, kt_ref, j_ref, inf_ref, d_ref, below_ref, above_ref, before_ref, after_ref,
    w_ref, both_ref, edge_ref, near_ref, g_ref, scal_ref, e_ref, f_ref,
):
    ev = lax.shift_right_logical(place_ref[0], 6)
    core = place_ref[0] & 1
    cube = to_cube(t_ref[...])
    square = apply_square(ev, d_ref, below_ref, above_ref, before_ref, after_ref, e_ref, f_ref)
    cube = [cube[i] + (damping * damping) * square[i] for i in range(8)]
    dd = jnp.zeros((32, 128), F32)
    dw = jnp.zeros((32, 128), F32)
    ww = jnp.zeros((32, 128), F32)
    for i in range(8):
        w_ref[i] = cube[i]
        d = d_ref[i]
        both_ref[i] = d
        both_ref[8 + i] = cube[i]
        dd = dd + d * d
        dw = dw + d * cube[i]
        ww = ww + cube[i] * cube[i]
    even = jnp.where(core == 0, 1.0, 0.0)
    edge_ref[0] = even * cube[0] + (1.0 - even) * cube[7]
    near_ref[0] = even * cube[7] + (1.0 - even) * cube[0]
    first = jnp.concatenate([cube[i][0:1] for i in range(8)], axis=0)
    last = jnp.concatenate([cube[i][31:32] for i in range(8)], axis=0)
    g_ref[2 * ((ev + 1) & 3) + core, 8:16] = last
    g_ref[2 * ((ev + 3) & 3) + core, 8:16] = first
    scal_ref[0:1] = jnp.sum(dd, axis=0, keepdims=True)
    scal_ref[1:2] = jnp.sum(dw, axis=0, keepdims=True)
    scal_ref[2:3] = jnp.sum(ww, axis=0, keepdims=True)
    whole = jnp.concatenate(
        [jnp.concatenate([cube[2 * i], cube[2 * i + 1]], axis=1) for i in range(4)], axis=0
    )
    gather_rays(whole, kt_ref, j_ref, inf_ref, g_ref)


def norms_kernel(place_ref, w_ref, edge_ref, near_ref, scal_ref, delay_ref, part_ref, out_ref, e_ref):
    ev = lax.shift_right_logical(place_ref[0], 6)
    core = place_ref[0] & 1
    even = jnp.where(core == 0, 1.0, 0.0)
    has_low = jnp.where(ev > 0, 1.0, 0.0)
    has_high = jnp.where(ev < 3, 1.0, 0.0)
    partner = near_ref[0]
    far = edge_ref[0]
    low = even * far + (1.0 - even) * partner
    high = even * partner + (1.0 - even) * far
    before = part_ref[2 * ((ev + 3) & 3) + core, 8:16] * has_low
    after = part_ref[2 * ((ev + 1) & 3) + core, 8:16] * has_high
    square = jnp.zeros((32, 128), F32)
    for i in range(8):
        x = w_ref[i]
        e_ref[8:40] = x
        e_ref[7:8] = before[i : i + 1]
        e_ref[40:41] = after[i : i + 1]
        left = low if i == 0 else w_ref[i - 1]
        right = high if i == 7 else w_ref[i + 1]
        value = 6.0 * x - (
            left + right + e_ref[7:39] + e_ref[9:41] + lane_neighbours(x, 1)
        )
        square = square + value * value
    lane = iota((1, 128), 1)
    b = delay_ref[...]
    numbers = [
        jnp.sum(scal_ref[0:1], axis=1, keepdims=True),
        jnp.sum(scal_ref[1:2], axis=1, keepdims=True),
        jnp.sum(scal_ref[2:3], axis=1, keepdims=True),
        jnp.sum(b * b, axis=1, keepdims=True),
        jnp.sum(jnp.sum(square, axis=0, keepdims=True), axis=1, keepdims=True),
    ]
    row = jnp.zeros((1, 128), F32)
    for n, number in enumerate(numbers):
        row = jnp.where(lane == n, number, row)
    total = part_ref[0, 0:8]
    for i in range(1, 8):
        total = total + part_ref[i, 0:8]
    for p in range(32):
        out_ref[9 * p : 9 * p + 8] = total
        out_ref[9 * p + 8 : 9 * p + 9] = row


def spread_kernel(x_ref, out_ref):
    total = x_ref[0]
    for i in range(1, x_ref.shape[0]):
        total = total + x_ref[i]
    for i in range(out_ref.shape[0]):
        out_ref[i] = total


def ray_norm_kernel(x_ref, out_ref):
    total = x_ref[0:8]
    row = x_ref[8:9]
    for p in range(1, 32):
        total = total + x_ref[9 * p : 9 * p + 8]
        row = row + x_ref[9 * p + 8 : 9 * p + 9]
    norm = jnp.sum(jnp.sum(total * total, axis=0, keepdims=True), axis=1, keepdims=True)
    row = jnp.where(iota((1, 128), 1) == 5, norm, row)
    out_ref[...] = jnp.broadcast_to(row, (8, 128))


def coefficient_kernel(scal_ref, out_ref):
    sums = jnp.sum(scal_ref[...], axis=0, keepdims=True)
    lane = iota((1, 128), 1)

    def number(n):
        return jnp.sum(jnp.where(lane == n, sums, 0.0), axis=1, keepdims=True)

    dd, dw, ww, bb = number(0), number(1), number(2), number(3)
    aa = number(5) + (damping * damping) * number(4)
    eps = norm_epsilon
    beta0 = jnp.sqrt(bb + eps)
    alpha0 = jnp.sqrt(dd / (beta0 * beta0) + eps)
    sigma0 = 1.0 / (beta0 * alpha0)
    ratio0 = alpha0 / beta0
    square1 = sigma0 * sigma0 * dw - 2.0 * sigma0 * ratio0 * dd + ratio0 * ratio0 * bb
    beta1 = jnp.sqrt(jnp.maximum(square1, 0.0) + eps)
    rho1 = jnp.sqrt(alpha0 * alpha0 + beta1 * beta1)
    cosine1, sine1 = alpha0 / rho1, beta1 / rho1
    phi1 = cosine1 * beta0
    phi_bar1 = sine1 * beta0
    shift = alpha0 * alpha0 + beta1 * beta1
    error2 = jnp.maximum(ww - 2.0 * shift * dw + shift * shift * dd, 0.0)
    scale1 = sigma0 / beta1
    alpha1 = jnp.sqrt(scale1 * scale1 * error2 + eps)
    tau = scale1 / alpha1
    theta1 = sine1 * alpha1
    rho_bar1 = -cosine1 * alpha1
    c1 = tau
    c0 = -tau * shift - alpha1 * sigma0 / beta1
    cb = alpha1 * ratio0 / beta1
    square2 = (
        c1 * c1 * aa
        + 2.0 * c1 * c0 * ww
        + c0 * c0 * dw
        + cb * cb * bb
        + 2.0 * c1 * cb * dw
        + 2.0 * c0 * cb * dd
    )
    beta2 = jnp.sqrt(jnp.maximum(square2, 0.0) + eps)
    rho2 = jnp.sqrt(rho_bar1 * rho_bar1 + beta2 * beta2)
    cosine2 = rho_bar1 / rho2
    phi2 = cosine2 * phi_bar1
    step = phi2 / rho2
    k1 = step * tau
    k0 = phi1 / rho1 * sigma0 - step * (tau * shift + theta1 / rho1 * sigma0)
    out_ref[0:1] = jnp.broadcast_to(k0, (1, 128))
    out_ref[1:2] = jnp.broadcast_to(k1, (1, 128))


def final_kernel(
    place_ref, k_ref, d0_ref, d1_ref, d3_ref, w0_ref, w1_ref, w3_ref, both_ref, out_ref, x_ref
):
    k0, k1 = k_ref[0:1], k_ref[1:2]
    ev = lax.shift_right_logical(place_ref[0], 6)
    for n in range(4):
        owner = (ev - n) & 3
        rows = pl.ds(pl.multiple_of(32 * owner, 32), 32)
        for i in range(8):
            if n == 2:
                d, w = both_ref[i], both_ref[8 + i]
            else:
                d_ref, w_ref = {0: (d0_ref, w0_ref), 1: (d1_ref, w1_ref), 3: (d3_ref, w3_ref)}[n]
                d, w = d_ref[i], w_ref[i]
            x_ref[i, rows, :] = k0 * d + k1 * w
    for i in range(8):
        out_ref[i] = x_ref[i].T


def exchange(x, axes):
    return lax.all_to_all(x, axes, split_axis=0, concat_axis=0, tiled=True)


def body(kernels, block_ids, delays):
    def ring(count, distance):
        return [(i, (i + distance) % count) for i in range(count)]

    def slab_shift(x, distance):
        return lax.ppermute(x, SLAB, ring(64, distance))

    def ev_shift(x, distance):
        return lax.ppermute(x, "ev", ring(4, distance))

    place = lax.axis_index(ALL).reshape(1)
    ev_spec = pl.BlockSpec(memory_space=pltpu.SMEM)

    def run_ev(body, args, out_shapes, scratch=()):
        outs = [jax.ShapeDtypeStruct(s, d) for s, d in out_shapes]
        return pl.pallas_call(
            body,
            out_shape=outs,
            in_specs=[ev_spec] + [VM] * len(args),
            out_specs=[VM] * len(outs),
            scratch_shapes=list(scratch),
            compiler_params=pltpu.CompilerParams(vmem_limit_bytes=16 << 20),
            cost_estimate=pl.CostEstimate(
                flops=1000000, bytes_accessed=1000000, transcendentals=0
            ),
        )(place, *args)

    send = pl.pallas_call(
        prep_kernel,
        out_shape=jax.ShapeDtypeStruct((1280, 128), F32),
        in_specs=[pl.BlockSpec(memory_space=pltpu.MemorySpace.HBM)] * 3,
        out_specs=VM,
        scratch_shapes=[
            pltpu.VMEM((1024, 1024), BF16),
            pltpu.VMEM((32, 32), I32),
            pltpu.VMEM((1, 32), F32),
            pltpu.VMEM((1024, 128), F32),
            pltpu.SemaphoreType.DMA((3,)),
        ],
        compiler_params=pltpu.CompilerParams(vmem_limit_bytes=16 << 20),
    )(
        pltpu.with_memory_space_constraint(block_ids, pltpu.MemorySpace.HBM),
        pltpu.with_memory_space_constraint(delays.reshape(1, 32), pltpu.MemorySpace.HBM),
        pltpu.with_memory_space_constraint(kernels.reshape(1024, 128), pltpu.MemorySpace.HBM),
    )
    received = exchange(send.reshape(256, 1, 640), ALL).reshape(1280, 128)

    cube = ((8, 32, 128), F32)
    d0, d_low, d_high, rays, kt, one_hot, info = run(
        first_kernel,
        (received,),
        [
            cube,
            ((2, 32, 128), F32),
            ((2, 32, 128), F32),
            ((8, 8, 128), F32),
            ((32, 4096), F32),
            ((256, 4096), BF16),
            ((64, 256), F32),
        ],
        [pltpu.VMEM((256, 4096), BF16)],
    )
    below = slab_shift(d_high, 1)
    above = slab_shift(d_low, -1)
    wide = jnp.concatenate([d0, above[:1], below[1:]], axis=0)
    d_1, d_3 = (ev_shift(wide, n) for n in (1, 3))

    rays = exchange(rays, D1)
    (rays,) = run(spread_kernel, (rays,), [((32, 8, 128), F32)])
    rays = exchange(rays, D2)
    (rays,) = run(spread_kernel, (rays,), [((8, 8, 128), F32)])
    rays = exchange(rays, D1)

    (applied,) = run(
        apply_kernel,
        (rays, kt, one_hot, info),
        [((128, 256), F32)],
        [pltpu.VMEM((256, 4096), BF16)],
    )
    w1, both, w_edge, w_near, rays1, scal = run_ev(
        second_kernel,
        (applied, kt, one_hot, info, d0, below, above, d_1, d_3),
        [cube, ((16, 32, 128), F32), ((1, 32, 128), F32), ((1, 32, 128), F32), ((8, 16, 128), F32), ((8, 128), F32)],
        [
            pltpu.VMEM((12, 48, 128), F32),
            pltpu.VMEM((12, 48, 128), F32),
        ],
    )
    pairs = [(i, (i + 1) % 64 if i % 2 else (i - 1) % 64) for i in range(64)]
    w_far = lax.ppermute(w_edge, SLAB, pairs)
    w_near = lax.ppermute(w_near, "sc", [(0, 1), (1, 0)])
    rays1 = exchange(rays1, NEAR)
    (packed,) = run_ev(
        norms_kernel,
        (w1, w_far, w_near, scal, delays.reshape(1, 32), rays1),
        [((288, 128), F32)],
        [pltpu.VMEM((48, 128), F32)],
    )
    w_1, w_3 = (ev_shift(w1, n) for n in (1, 3))
    both_2 = ev_shift(both, 2)
    packed = exchange(packed.reshape(32, 1, 1152), FAR).reshape(288, 128)
    (sums,) = run(ray_norm_kernel, (packed,), [((8, 128), F32)])
    sums = exchange(sums.reshape(8, 1, 128), NEAR).reshape(8, 128)
    (coefs,) = run(coefficient_kernel, (sums,), [((8, 128), F32)])
    (out,) = run_ev(
        final_kernel,
        (coefs, d0, d_1, d_3, w1, w_1, w_3, both_2),
        [((8, 128, 128), F32)],
        [pltpu.VMEM((8, 128, 128), F32)],
    )
    return out


def solution(mesh):
    fine = Mesh(mesh.devices.reshape(4, 4, 8, 2), ALL)
    rays = P(ALL)
    return jax.shard_map(
        body, mesh=fine, in_specs=(rays, rays, rays), out_specs=P(SLAB), check_vma=False
    )
```

```python
import jax
import jax.numpy as jnp
from jax import lax
from jax.experimental import pallas as pl
from jax.experimental.pallas import tpu as pltpu
from jax.sharding import Mesh, PartitionSpec as P

damping = 0.3
norm_epsilon = 1e-06

F32 = jnp.float32
BF16 = jnp.bfloat16
I32 = jnp.int32


ALL = ("ev", "sx", "sz", "sc")
SLAB = ("sx", "sz", "sc")
D1 = ("sx", "sc")
D2 = ("ev", "sz")
NEAR = ("ev", "sc")
FAR = ("sx", "sz")

VM = pl.BlockSpec(memory_space=pltpu.VMEM)


def iota(shape, dim):
    return lax.broadcasted_iota(I32, shape, dim)


def split2(x):
    hi = x.astype(BF16)
    return hi, (x - hi.astype(F32)).astype(BF16)


def run(body, args, out_shapes, scratch=(), flops=1000000, nbytes=1000000):
    outs = [jax.ShapeDtypeStruct(s, d) for s, d in out_shapes]
    return pl.pallas_call(
        body,
        out_shape=outs,
        in_specs=[VM] * len(args),
        out_specs=[VM] * len(outs),
        scratch_shapes=list(scratch),
        compiler_params=pltpu.CompilerParams(vmem_limit_bytes=16 << 20),
        cost_estimate=pl.CostEstimate(flops=flops, bytes_accessed=nbytes, transcendentals=0),
    )(*args)


def prep_kernel(ids_hbm, b_hbm, k_hbm, send_ref, oh_ref, ids_ref, b_ref, k_ref, sem):
    ids_copy = pltpu.make_async_copy(ids_hbm, ids_ref, sem.at[0])
    b_copy = pltpu.make_async_copy(b_hbm, b_ref, sem.at[1])
    copy = pltpu.make_async_copy(k_hbm, k_ref, sem.at[2])
    ids_copy.start()
    b_copy.start()
    copy.start()
    entry = iota((32, 1024), 1)
    sub = iota((32, 1024), 0)
    spread_k = jnp.where((entry & 31) == sub, 1.0, 0.0).astype(BF16)
    spread_ray = jnp.where(lax.shift_right_logical(entry, 5) == sub, 1.0, 0.0)
    ids_copy.wait()
    b_copy.wait()
    ids2 = ids_ref[...]
    halves = jnp.concatenate(
        [lax.shift_right_logical(ids2, 8).astype(F32), (ids2 & 255).astype(F32)], axis=0
    )
    halves = jnp.dot(halves.astype(BF16), spread_k, preferred_element_type=F32)
    ids = jnp.sum((halves[:32] * 256.0 + halves[32:]) * spread_ray, axis=0, keepdims=True)
    ids = ids.astype(I32)
    b = b_ref[...]
    b_hi = b.astype(BF16)
    b_mid, b_lo = split2(b - b_hi.astype(F32))
    b_rows = jnp.concatenate([jnp.broadcast_to(v, (16, 32)) for v in (b_hi, b_mid, b_lo)], axis=0)
    b_rows = jnp.dot(b_rows, spread_ray.astype(BF16), preferred_element_type=F32).astype(BF16)
    slab = lax.shift_right_logical(ids, 10)
    loc = ids & 1023
    s_f = (iota((64, 1024), 0) == slab).astype(F32)
    s_b = s_f.astype(BF16)
    ra, ca = iota((128, 256), 0), iota((128, 256), 1)
    upper = jnp.where((ra < ca) | (ca >= 128), 1.0, 0.0).astype(BF16)
    stacked = jnp.concatenate([s_b[:, 128 * i : 128 * i + 128] for i in range(8)], axis=0)
    counts = jnp.dot(stacked, upper, preferred_element_type=F32)
    offset = jnp.zeros((64, 128), F32)
    ranks = []
    for i in range(8):
        block = counts[64 * i : 64 * i + 64]
        ranks.append(
            jnp.sum(
                s_f[:, 128 * i : 128 * i + 128] * (block[:, :128] + offset), axis=0, keepdims=True
            )
        )
        offset = offset + block[:, 128:]
    rank = jnp.concatenate(ranks, axis=1)
    for m in range(4):
        for r in range(4):
            pick = jnp.where(rank == float(4 * r + m), 1.0, 0.0).astype(BF16)
            oh_ref[64 * (4 * m + r) : 64 * (4 * m + r) + 64, :] = s_b * pick
    copy.wait()
    k_hi, k_lo = split2(k_ref[...])
    both = jnp.dot(
        oh_ref[...], jnp.concatenate([k_hi, k_lo], axis=1), preferred_element_type=F32
    )
    perm = both[:, :128] + both[:, 128:]
    lane_block = lax.shift_right_logical(iota((64, 128), 1), 5)
    for r in range(4):
        rows = [perm[64 * (4 * m + r) : 64 * (4 * m + r) + 64] for m in range(4)]
        for e in range(4):
            value = None
            for m in range(4):
                d = (m - e) % 4
                moved = rows[m] if d == 0 else pltpu.roll(rows[m], 32 * d, axis=1)
                value = moved if value is None else jnp.where(lane_block == m, moved, value)
            send_ref[pl.ds(320 * e + r, 64, stride=5), :] = value
    loc_i = lax.shift_right_logical(loc, 7)
    group = lax.shift_right_logical(loc_i, 1).astype(F32)
    column = ((loc_i & 1) * 128 + (loc & 127)).astype(F32)
    ray = lax.shift_right_logical(iota((1, 1024), 1), 5).astype(F32)
    b_parts = [b_rows[16 * i : 16 * i + 1] for i in range(3)]
    values = [group.astype(BF16), column.astype(BF16), ray.astype(BF16)] + b_parts
    left = jnp.concatenate([s_b * v for v in values], axis=0)
    slot = (iota((128, 1024), 0) & 15).astype(F32)
    right = jnp.where(slot == rank, 1.0, 0.0).astype(BF16)
    info = lax.dot_general(left, right, (((1,), (1,)), ((), ())), preferred_element_type=F32)
    lane16 = lax.shift_right_logical(iota((64, 128), 1), 4)
    b_info = info[192:256] + info[256:320] + info[320:384]
    merged = jnp.where(
        lane16 == 0,
        info[0:64],
        jnp.where(lane16 == 1, info[64:128], jnp.where(lane16 == 2, info[128:192], b_info)),
    )
    for e in range(4):
        send_ref[pl.ds(320 * e + 4, 64, stride=5), :] = merged


def scatter_rows(kt_ref, j_ref, inf_ref, l_ref, weight_rows):
    for t in range(16):
        cols = slice(256 * t, 256 * t + 256)
        w_hi, w_lo = split2(kt_ref[:, cols] * weight_rows[t])
        group = inf_ref[t : t + 1, :]
        for i in range(4):
            mask = jnp.where(group == float(i), 1.0, 0.0).astype(BF16)
            l_ref[32 * i : 32 * i + 32, cols] = w_hi * mask
            l_ref[128 + 32 * i : 160 + 32 * i, cols] = w_lo * mask
    acc = lax.dot_general(
        l_ref[...], j_ref[...], (((1,), (1,)), ((), ())), preferred_element_type=F32
    )
    return acc[:128] + acc[128:]


def to_cube(flat):
    return [
        flat[32 * (i // 2) : 32 * (i // 2) + 32, 128 * (i % 2) : 128 * (i % 2) + 128]
        for i in range(8)
    ]


def gather_rays(flat, kt_ref, j_ref, inf_ref, g_ref):
    parts = jnp.concatenate(split2(flat), axis=0)
    ray_index = iota((32, 256), 0).astype(F32)
    total = jnp.zeros((32, 256), F32)
    for t in range(16):
        cols = slice(256 * t, 256 * t + 256)
        picked = jnp.dot(parts, j_ref[:, cols], preferred_element_type=F32)
        group = inf_ref[t : t + 1, :]
        value = jnp.zeros((32, 256), F32)
        for i in range(4):
            both = picked[32 * i : 32 * i + 32] + picked[128 + 32 * i : 160 + 32 * i]
            value = jnp.where(group == float(i), both, value)
        entry = jnp.sum(kt_ref[:, cols] * value, axis=0, keepdims=True)
        total = total + jnp.where(inf_ref[32 + t : 33 + t, :] == ray_index, entry, 0.0)
    for a in range(4):
        for h in range(2):
            g_ref[2 * a + h, 0:8] = total[8 * a : 8 * a + 8, 128 * h : 128 * h + 128]


def first_kernel(place_ref, r_ref, d_ref, far_ref, near_ref, g_ref, kt_ref, j_ref, inf_ref, l_ref):
    inf_ref[...] = r_ref[pl.ds(4, 256, stride=5), :].T[:64]
    for r in range(4):
        block = r_ref[pl.ds(r, 256, stride=5), :].T
        for m in range(4):
            t = 4 * r + m
            kt_ref[:, 256 * t : 256 * t + 256] = block[32 * m : 32 * m + 32]
    row = iota((256, 256), 0).astype(F32)
    for t in range(16):
        hit = jnp.where(row == inf_ref[16 + t : 17 + t, :], 1.0, 0.0)
        j_ref[:, 256 * t : 256 * t + 256] = hit.astype(BF16)
    flat = scatter_rows(
        kt_ref, j_ref, inf_ref, l_ref, [inf_ref[48 + t : 49 + t, :] for t in range(16)]
    )
    cube = to_cube(flat)
    for i in range(8):
        d_ref[i] = cube[i]
    even = (place_ref[0] & 1) == 0
    for i in range(2):
        far_ref[i] = jnp.where(even, cube[i], cube[6 + i])
        near_ref[i] = jnp.where(even, cube[6 + i], cube[i])
    gather_rays(flat, kt_ref, j_ref, inf_ref, g_ref)


def lane_neighbours(x, axis):
    size = x.shape[axis]
    lane = lax.broadcasted_iota(I32, x.shape, axis)
    up = jnp.where(lane == 0, 0.0, pltpu.roll(x, 1, axis=axis))
    down = jnp.where(lane == size - 1, 0.0, pltpu.roll(x, size - 1, axis=axis))
    return up + down


def apply_square(ev, core, d_ref, far_ref, near_ref, before_ref, after_ref, e_ref, f_ref):
    has_low = jnp.where(ev > 0, 1.0, 0.0)
    has_high = jnp.where(ev < 3, 1.0, 0.0)
    for i in range(12):
        if i < 2:
            own = jnp.where(core == 0, far_ref[i], near_ref[i])
        elif i < 10:
            own = d_ref[i - 2]
        else:
            own = jnp.where(core == 0, near_ref[i - 10], far_ref[i - 10])
        e_ref[i, 8:40] = own
    for i in range(12):
        e_ref[i, 0:8] = jnp.zeros((8, 128), F32)
        e_ref[i, 40:48] = jnp.zeros((8, 128), F32)
    for i in range(1, 11):
        n = 9 if i == 1 else i - 2
        for c in range(2):
            e_ref[i, 6 + c : 7 + c] = before_ref[c, n : n + 1] * has_low
            e_ref[i, 40 + c : 41 + c] = after_ref[c, n : n + 1] * has_high
    radial = iota((48, 128), 0)
    inside = jnp.where(radial < 8, has_low, jnp.where(radial >= 40, has_high, 1.0))

    def laplace(ref, i):
        x = ref[i]
        radial_sum = pltpu.roll(x, 1, axis=0) + pltpu.roll(x, 47, axis=0)
        return 6.0 * x - (ref[i - 1] + ref[i + 1] + radial_sum + lane_neighbours(x, 1))

    for i in range(1, 11):
        f_ref[i] = laplace(e_ref, i) * inside
    return [laplace(f_ref, i)[8:40] for i in range(2, 10)]


def strip_kernel(place_ref, d_ref, far_ref, near_ref, low_ref, high_ref):
    even = (place_ref[0] & 1) == 0
    above = jnp.where(even, near_ref[0], far_ref[0])
    below = jnp.where(even, far_ref[1], near_ref[1])
    for c in range(2):
        for n in range(16):
            if n < 8:
                source = d_ref[n]
            else:
                source = above if n == 8 else below
            low_ref[c, n : n + 1] = source[c : c + 1]
            high_ref[c, n : n + 1] = source[30 + c : 31 + c]


def apply_kernel(g0_ref, kt_ref, j_ref, inf_ref, t_ref, l_ref):
    rays = jnp.concatenate(
        [jnp.concatenate([g0_ref[2 * a], g0_ref[2 * a + 1]], axis=1) for a in range(4)], axis=0
    )
    ray_index = iota((32, 256), 0).astype(F32)
    weights = [
        jnp.sum(
            jnp.where(inf_ref[32 + t : 33 + t, :] == ray_index, rays, 0.0), axis=0, keepdims=True
        )
        for t in range(16)
    ]
    t_ref[...] = scatter_rows(kt_ref, j_ref, inf_ref, l_ref, weights)


def second_kernel(
    place_ref, t_ref, kt_ref, j_ref, inf_ref, d_ref, far_ref, near_in_ref, before_ref, after_ref,
    w_ref, both_ref, edge_ref, near_ref, g_ref, scal_ref, e_ref, f_ref,
):
    ev = lax.shift_right_logical(place_ref[0], 6)
    core = place_ref[0] & 1
    cube = to_cube(t_ref[...])
    square = apply_square(ev, core, d_ref, far_ref, near_in_ref, before_ref, after_ref, e_ref, f_ref)
    cube = [cube[i] + (damping * damping) * square[i] for i in range(8)]
    dd = jnp.zeros((32, 128), F32)
    dw = jnp.zeros((32, 128), F32)
    ww = jnp.zeros((32, 128), F32)
    for i in range(8):
        w_ref[i] = cube[i]
        d = d_ref[i]
        both_ref[i] = d
        both_ref[8 + i] = cube[i]
        dd = dd + d * d
        dw = dw + d * cube[i]
        ww = ww + cube[i] * cube[i]
    even = jnp.where(core == 0, 1.0, 0.0)
    edge_ref[0] = even * cube[0] + (1.0 - even) * cube[7]
    near_ref[0] = even * cube[7] + (1.0 - even) * cube[0]
    first = jnp.concatenate([cube[i][0:1] for i in range(8)], axis=0)
    last = jnp.concatenate([cube[i][31:32] for i in range(8)], axis=0)
    g_ref[2 * ((ev + 1) & 3) + core, 8:16] = last
    g_ref[2 * ((ev + 3) & 3) + core, 8:16] = first
    scal_ref[0:1] = jnp.sum(dd, axis=0, keepdims=True)
    scal_ref[1:2] = jnp.sum(dw, axis=0, keepdims=True)
    scal_ref[2:3] = jnp.sum(ww, axis=0, keepdims=True)
    whole = jnp.concatenate(
        [jnp.concatenate([cube[2 * i], cube[2 * i + 1]], axis=1) for i in range(4)], axis=0
    )
    gather_rays(whole, kt_ref, j_ref, inf_ref, g_ref)


def norms_kernel(place_ref, w_ref, edge_ref, near_ref, scal_ref, delay_ref, part_ref, out_ref, e_ref):
    ev = lax.shift_right_logical(place_ref[0], 6)
    core = place_ref[0] & 1
    even = jnp.where(core == 0, 1.0, 0.0)
    has_low = jnp.where(ev > 0, 1.0, 0.0)
    has_high = jnp.where(ev < 3, 1.0, 0.0)
    partner = near_ref[0]
    far = edge_ref[0]
    low = even * far + (1.0 - even) * partner
    high = even * partner + (1.0 - even) * far
    before = part_ref[2 * ((ev + 3) & 3) + core, 8:16] * has_low
    after = part_ref[2 * ((ev + 1) & 3) + core, 8:16] * has_high
    square = jnp.zeros((32, 128), F32)
    for i in range(8):
        x = w_ref[i]
        e_ref[8:40] = x
        e_ref[7:8] = before[i : i + 1]
        e_ref[40:41] = after[i : i + 1]
        left = low if i == 0 else w_ref[i - 1]
        right = high if i == 7 else w_ref[i + 1]
        value = 6.0 * x - (
            left + right + e_ref[7:39] + e_ref[9:41] + lane_neighbours(x, 1)
        )
        square = square + value * value
    lane = iota((1, 128), 1)
    b = delay_ref[...]
    numbers = [
        jnp.sum(scal_ref[0:1], axis=1, keepdims=True),
        jnp.sum(scal_ref[1:2], axis=1, keepdims=True),
        jnp.sum(scal_ref[2:3], axis=1, keepdims=True),
        jnp.sum(b * b, axis=1, keepdims=True),
        jnp.sum(jnp.sum(square, axis=0, keepdims=True), axis=1, keepdims=True),
    ]
    row = jnp.zeros((1, 128), F32)
    for n, number in enumerate(numbers):
        row = jnp.where(lane == n, number, row)
    total = part_ref[0, 0:8]
    for i in range(1, 8):
        total = total + part_ref[i, 0:8]
    for p in range(32):
        out_ref[9 * p : 9 * p + 8] = total
        out_ref[9 * p + 8 : 9 * p + 9] = row


def spread_kernel(x_ref, out_ref):
    total = x_ref[0]
    for i in range(1, x_ref.shape[0]):
        total = total + x_ref[i]
    for i in range(out_ref.shape[0]):
        out_ref[i] = total


def ray_norm_kernel(x_ref, out_ref):
    total = x_ref[0:8]
    row = x_ref[8:9]
    for p in range(1, 32):
        total = total + x_ref[9 * p : 9 * p + 8]
        row = row + x_ref[9 * p + 8 : 9 * p + 9]
    norm = jnp.sum(jnp.sum(total * total, axis=0, keepdims=True), axis=1, keepdims=True)
    row = jnp.where(iota((1, 128), 1) == 5, norm, row)
    out_ref[...] = jnp.broadcast_to(row, (8, 128))


def coefficient_kernel(scal_ref, out_ref):
    sums = jnp.sum(scal_ref[...], axis=0, keepdims=True)
    lane = iota((1, 128), 1)

    def number(n):
        return jnp.sum(jnp.where(lane == n, sums, 0.0), axis=1, keepdims=True)

    dd, dw, ww, bb = number(0), number(1), number(2), number(3)
    aa = number(5) + (damping * damping) * number(4)
    eps = norm_epsilon
    beta0 = jnp.sqrt(bb + eps)
    alpha0 = jnp.sqrt(dd / (beta0 * beta0) + eps)
    sigma0 = 1.0 / (beta0 * alpha0)
    ratio0 = alpha0 / beta0
    square1 = sigma0 * sigma0 * dw - 2.0 * sigma0 * ratio0 * dd + ratio0 * ratio0 * bb
    beta1 = jnp.sqrt(jnp.maximum(square1, 0.0) + eps)
    rho1 = jnp.sqrt(alpha0 * alpha0 + beta1 * beta1)
    cosine1, sine1 = alpha0 / rho1, beta1 / rho1
    phi1 = cosine1 * beta0
    phi_bar1 = sine1 * beta0
    shift = alpha0 * alpha0 + beta1 * beta1
    error2 = jnp.maximum(ww - 2.0 * shift * dw + shift * shift * dd, 0.0)
    scale1 = sigma0 / beta1
    alpha1 = jnp.sqrt(scale1 * scale1 * error2 + eps)
    tau = scale1 / alpha1
    theta1 = sine1 * alpha1
    rho_bar1 = -cosine1 * alpha1
    c1 = tau
    c0 = -tau * shift - alpha1 * sigma0 / beta1
    cb = alpha1 * ratio0 / beta1
    square2 = (
        c1 * c1 * aa
        + 2.0 * c1 * c0 * ww
        + c0 * c0 * dw
        + cb * cb * bb
        + 2.0 * c1 * cb * dw
        + 2.0 * c0 * cb * dd
    )
    beta2 = jnp.sqrt(jnp.maximum(square2, 0.0) + eps)
    rho2 = jnp.sqrt(rho_bar1 * rho_bar1 + beta2 * beta2)
    cosine2 = rho_bar1 / rho2
    phi2 = cosine2 * phi_bar1
    step = phi2 / rho2
    k1 = step * tau
    k0 = phi1 / rho1 * sigma0 - step * (tau * shift + theta1 / rho1 * sigma0)
    out_ref[0:1] = jnp.broadcast_to(k0, (1, 128))
    out_ref[1:2] = jnp.broadcast_to(k1, (1, 128))


def final_kernel(
    place_ref, k_ref, d_ref, w_ref, both1_ref, both2_ref, both3_ref, out_ref, x_ref
):
    k0, k1 = k_ref[0:1], k_ref[1:2]
    ev = lax.shift_right_logical(place_ref[0], 6)
    rows = pl.ds(pl.multiple_of(32 * ev, 32), 32)
    for i in range(8):
        x_ref[i, rows, :] = k0 * d_ref[i] + k1 * w_ref[i]
    for n, both_ref in ((1, both1_ref), (2, both2_ref), (3, both3_ref)):
        rows = pl.ds(pl.multiple_of(32 * ((ev - n) & 3), 32), 32)
        for i in range(8):
            x_ref[i, rows, :] = k0 * both_ref[i] + k1 * both_ref[8 + i]
    for i in range(8):
        out_ref[i] = x_ref[i].T


def exchange(x, axes):
    return lax.all_to_all(x, axes, split_axis=0, concat_axis=0, tiled=True)


def body(kernels, block_ids, delays):
    def ring(count, distance):
        return [(i, (i + distance) % count) for i in range(count)]

    def ev_shift(x, distance):
        return lax.ppermute(x, "ev", ring(4, distance))

    place = lax.axis_index(ALL).reshape(1)
    ev_spec = pl.BlockSpec(memory_space=pltpu.SMEM)

    def run_ev(body, args, out_shapes, scratch=()):
        outs = [jax.ShapeDtypeStruct(s, d) for s, d in out_shapes]
        return pl.pallas_call(
            body,
            out_shape=outs,
            in_specs=[ev_spec] + [VM] * len(args),
            out_specs=[VM] * len(outs),
            scratch_shapes=list(scratch),
            compiler_params=pltpu.CompilerParams(vmem_limit_bytes=16 << 20),
            cost_estimate=pl.CostEstimate(
                flops=1000000, bytes_accessed=1000000, transcendentals=0
            ),
        )(place, *args)

    send = pl.pallas_call(
        prep_kernel,
        out_shape=jax.ShapeDtypeStruct((1280, 128), F32),
        in_specs=[pl.BlockSpec(memory_space=pltpu.MemorySpace.HBM)] * 3,
        out_specs=VM,
        scratch_shapes=[
            pltpu.VMEM((1024, 1024), BF16),
            pltpu.VMEM((32, 32), I32),
            pltpu.VMEM((1, 32), F32),
            pltpu.VMEM((1024, 128), F32),
            pltpu.SemaphoreType.DMA((3,)),
        ],
        compiler_params=pltpu.CompilerParams(vmem_limit_bytes=16 << 20),
    )(
        pltpu.with_memory_space_constraint(block_ids, pltpu.MemorySpace.HBM),
        pltpu.with_memory_space_constraint(delays.reshape(1, 32), pltpu.MemorySpace.HBM),
        pltpu.with_memory_space_constraint(kernels.reshape(1024, 128), pltpu.MemorySpace.HBM),
    )
    received = exchange(send.reshape(256, 1, 640), ALL).reshape(1280, 128)

    cube = ((8, 32, 128), F32)
    d0, d_far, d_near, rays, kt, one_hot, info = run_ev(
        first_kernel,
        (received,),
        [
            cube,
            ((2, 32, 128), F32),
            ((2, 32, 128), F32),
            ((8, 8, 128), F32),
            ((32, 4096), F32),
            ((256, 4096), BF16),
            ((64, 256), F32),
        ],
        [pltpu.VMEM((256, 4096), BF16)],
    )
    far_pairs = [(i, (i + 1) % 64 if i % 2 else (i - 1) % 64) for i in range(64)]
    near_pairs = [(0, 1), (1, 0)]
    d_far = lax.ppermute(d_far, SLAB, far_pairs)
    d_near = lax.ppermute(d_near, "sc", near_pairs)
    rays = exchange(rays, D1)
    (rays,) = run(spread_kernel, (rays,), [((32, 8, 128), F32)])
    rays = exchange(rays, D2)
    (rays,) = run(spread_kernel, (rays,), [((8, 8, 128), F32)])
    low, high = run_ev(strip_kernel, (d0, d_far, d_near), [((2, 16, 128), F32)] * 2)
    before = ev_shift(high, 1)
    after = ev_shift(low, -1)
    rays = exchange(rays, D1)

    (applied,) = run(
        apply_kernel,
        (rays, kt, one_hot, info),
        [((128, 256), F32)],
        [pltpu.VMEM((256, 4096), BF16)],
    )
    w1, both, w_edge, w_near, rays1, scal = run_ev(
        second_kernel,
        (applied, kt, one_hot, info, d0, d_far, d_near, before, after),
        [cube, ((16, 32, 128), F32), ((1, 32, 128), F32), ((1, 32, 128), F32), ((8, 16, 128), F32), ((8, 128), F32)],
        [
            pltpu.VMEM((12, 48, 128), F32),
            pltpu.VMEM((12, 48, 128), F32),
        ],
    )
    w_far = lax.ppermute(w_edge, SLAB, far_pairs)
    w_near = lax.ppermute(w_near, "sc", near_pairs)
    rays1 = exchange(rays1, NEAR)
    (packed,) = run_ev(
        norms_kernel,
        (w1, w_far, w_near, scal, delays.reshape(1, 32), rays1),
        [((288, 128), F32)],
        [pltpu.VMEM((48, 128), F32)],
    )
    both_1, both_2, both_3 = (ev_shift(both, n) for n in (1, 2, 3))
    packed = exchange(packed.reshape(32, 1, 1152), FAR).reshape(288, 128)
    (sums,) = run(ray_norm_kernel, (packed,), [((8, 128), F32)])
    sums = exchange(sums.reshape(8, 1, 128), NEAR).reshape(8, 128)
    (coefs,) = run(coefficient_kernel, (sums,), [((8, 128), F32)])
    (out,) = run_ev(
        final_kernel,
        (coefs, d0, w1, both_1, both_2, both_3),
        [((8, 128, 128), F32)],
        [pltpu.VMEM((8, 128, 128), F32)],
    )
    return out


def solution(mesh):
    fine = Mesh(mesh.devices.reshape(4, 4, 8, 2), ALL)
    rays = P(ALL)
    return jax.shard_map(
        body, mesh=fine, in_specs=(rays, rays, rays), out_specs=P(SLAB), check_vma=False
    )
```
